1024 devices in a mesh: gx: 8 (over x), gy: 8 (over y), gz: 16 (over z, core).
Axes of the slice: x: 8, y: 8, z: 8, core: 2. Of those that a mesh axis runs over, the one named last changes fastest.
Arguments:
- loads: float32 [8, 8, 16, 12, 768], P('gx', 'gy', 'gz')
- dual_ops: bfloat16 [8, 8, 16, 768, 768], P('gx', 'gy', 'gz'), as said below
- precond: bfloat16 [8, 8, 16, 768, 768], P('gx', 'gy', 'gz'), as said below
- counts: int32 [8, 8, 16, 18], P('gx', 'gy', 'gz'), may hold values from 0 to 96, as said below
- signs: int32 [8, 8, 16, 768], P('gx', 'gy', 'gz'), may hold values from -1 to 1, as said below
Outputs:
- multipliers: float32 [8, 8, 16, 12, 768], P('gx', 'gy', 'gz')
- residual: float32 [8, 8, 16, 12, 768], P('gx', 'gy', 'gz')
The draws below stay inside these ranges and needn't reach their ends.
Inputs may be any that keep to these rules, and one draw needn't show every extreme that they name: counts[s, d] equals counts[s + offset(d), opp(d)] and is 0 where s + offset(d) lies outside the grid; inside, a face block holds 48 to 96 live multipliers and an edge block 8 to 16, and both bounds 96 and 16 are reached; live slots are the first ones of their block. `signs`: every entry is -1 or 1. `dual_ops`: each subdomain's matrix is symmetric and positive definite. `precond`: each subdomain's matrix is symmetric and positive definite.
All inputs are finite; a program needn't handle non-finite values.
Results may differ from the reference program's by a relative error of at most 0.0055.
The reference program's roundings to bfloat16 on the way count: a program that leaves them out, or rounds other values in their place, can miss the bound.
Values sent between devices are 32-bit elements; how exact they have to be, the bound alone decides.
No kernel may reach another device: no remote copies, remote signals or barrier semaphores. Data moves between devices by JAX's collectives and lax.ppermute only.
A program may use at most 32 MiB of HBM per device.

```python
import math
import jax
import jax.numpy as jnp
import numpy as np
from jax import lax

FACE = 96
EDGE = 16
CASES = 12
ITERS = 2
NX = 8
NY = 8
NZ = 16


DIRECTIONS = ((1, 0, 0), (-1, 0, 0), (0, 1, 0), (0, -1, 0), (0, 0, 1), (0, 0, -1), (1, 1, 0), (1, -1, 0), (-1, 1, 0), (-1, -1, 0), (1, 0, 1), (1, 0, -1), (-1, 0, 1), (-1, 0, -1), (0, 1, 1), (0, 1, -1), (0, -1, 1), (0, -1, -1))


def symmetric_blocks(key, diagonal_low, diagonal_high, spread):
    order_max = 6 * FACE + 12 * EDGE
    subdomains = NX * NY * NZ

    def single(number):
        subkey = jax.random.fold_in(key, number)
        key_entries, key_diagonal = jax.random.split(subkey)
        random_part = jax.random.normal(key_entries, (order_max, order_max), jnp.float32)
        symmetric = (random_part + random_part.T) * (spread / math.sqrt(2.0 * order_max))
        diagonal = jax.random.uniform(key_diagonal, (order_max,), jnp.float32, diagonal_low, diagonal_high)
        return (symmetric + jnp.diag(diagonal)).astype(jnp.bfloat16)
    blocks = lax.map(single, jnp.arange(subdomains, dtype=jnp.int32))
    return blocks.reshape(NX, NY, NZ, order_max, order_max)


def draw_dual_ops(key, part):
    return symmetric_blocks(jax.random.fold_in(key, 11), 1.6, 2.4, 0.6)


def draw_precond(key, part):
    return symmetric_blocks(jax.random.fold_in(key, 23), 1.4, 2.2, 0.5)


def draw_loads(key, part):
    order_max = 6 * FACE + 12 * EDGE
    key_base, key_scale, key_common = jax.random.split(jax.random.fold_in(key, 31), 3)
    shape = (NX, NY, NZ, CASES, order_max)
    rising = 1.0 + 2.0 * jnp.arange(NZ, dtype=jnp.float32) / (NZ - 1.0)
    rising = rising[None, None, :, None, None]
    values = jax.random.normal(key_base, shape, jnp.float32)
    scales = jnp.exp(jax.random.uniform(key_scale, (NX, NY, NZ, CASES, 1), jnp.float32, 0.0, math.log(4.0)))
    return values * scales * rising


def draw_signs(key, part):
    order_max = 6 * FACE + 12 * EDGE
    drawn = jax.random.randint(jax.random.fold_in(key, 41), (NX, NY, NZ, order_max), 0, 2, dtype=jnp.int32)
    return 2 * drawn - 1


def draw_counts(key, part):
    grid_x = jnp.arange(NX, dtype=jnp.int32)[:, None, None]
    grid_y = jnp.arange(NY, dtype=jnp.int32)[None, :, None]
    grid_z = jnp.arange(NZ, dtype=jnp.int32)[None, None, :]

    def inside(heading):
        shifted_x = grid_x + heading[0]
        shifted_y = grid_y + heading[1]
        shifted_z = grid_z + heading[2]
        return (shifted_x >= 0) & (shifted_x < NX) & (shifted_y >= 0) & (shifted_y < NY) & (shifted_z >= 0) & (shifted_z < NZ)
    columns = [None] * 18
    for course, heading in enumerate(DIRECTIONS):
        leading = [value for value in heading if value != 0][0]
        if leading < 0:
            continue
        capacity = FACE if course < 6 else EDGE
        drawn = jax.random.randint(jax.random.fold_in(key, 100 + course), (NX, NY, NZ), capacity // 2, capacity + 1, dtype=jnp.int32)
        corner = tuple((0 if value >= 0 else 1 for value in heading))
        drawn = drawn.at[corner].set(capacity)
        forward = jnp.where(inside(heading), drawn, 0)
        reverse = (-heading[0], -heading[1], -heading[2])
        backward = jnp.where(inside(reverse), jnp.roll(drawn, shift=heading, axis=(0, 1, 2)), 0)
        columns[course] = forward.astype(jnp.int32)
        columns[DIRECTIONS.index(reverse)] = backward.astype(jnp.int32)
    return jnp.stack(columns, axis=-1)


def setup_inputs(seed: int = 0) -> dict:
    streams_of = jax.random.split(jax.random.key(seed), 6)
    return {
        "loads": draw_loads(jax.random.fold_in(streams_of[5], 71), 0),
        "dual_ops": draw_dual_ops(jax.random.fold_in(streams_of[5], 71), 0),
        "precond": draw_precond(jax.random.fold_in(streams_of[5], 71), 0),
        "counts": draw_counts(jax.random.fold_in(streams_of[5], 71), 0),
        "signs": draw_signs(jax.random.fold_in(streams_of[5], 71), 0),
    }


DIRECTIONS = ((1, 0, 0), (-1, 0, 0), (0, 1, 0), (0, -1, 0), (0, 0, 1), (0, 0, -1),
              (1, 1, 0), (1, -1, 0), (-1, 1, 0), (-1, -1, 0), (1, 0, 1), (1, 0, -1),
              (-1, 0, 1), (-1, 0, -1), (0, 1, 1), (0, 1, -1), (0, -1, 1), (0, -1, -1))


def opposite(course):
    heading = DIRECTIONS[course]
    return DIRECTIONS.index((-heading[0], -heading[1], -heading[2]))


def block_table():
    capacity = [FACE] * 6 + [EDGE] * 12
    offsets = [sum(capacity[:course]) for course in range(18)]
    return capacity, offsets


def live_slots(counts):
    capacity, offsets = block_table()
    order_max = sum(capacity)
    owners = np.zeros((18, order_max), np.int32)
    position = np.zeros((order_max,), np.int32)
    for course in range(18):
        owners[course, offsets[course]:offsets[course] + capacity[course]] = 1
        position[offsets[course]:offsets[course] + capacity[course]] = np.arange(capacity[course])
    limits = jnp.sum(counts[..., :, None] * jnp.asarray(owners, jnp.int32), axis=-2)
    return (jnp.asarray(position, jnp.int32) < limits).astype(jnp.float32)


def neighbour_blocks(contribution):
    capacity, offsets = block_table()
    padded = jnp.pad(contribution, ((1, 1), (1, 1), (1, 1), (0, 0), (0, 0)))
    pieces = []
    for course, heading in enumerate(DIRECTIONS):
        back = opposite(course)
        nearby = padded[1 + heading[0]:1 + heading[0] + NX, 1 + heading[1]:1 + heading[1] + NY,
                        1 + heading[2]:1 + heading[2] + NZ]
        pieces.append(nearby[..., offsets[back]:offsets[back] + capacity[back]])
    return jnp.concatenate(pieces, axis=-1)


def apply_local(matrices, signed, vector):
    order_max = vector.shape[-1]
    scaled = (signed[..., None, :] * vector).astype(jnp.bfloat16).reshape(-1, CASES, order_max)
    flattened = matrices.reshape(-1, order_max, order_max)

    def single(operands):
        return jnp.dot(operands[0], operands[1], preferred_element_type=jnp.float32)

    product = lax.map(single, (scaled, flattened))
    return signed[..., None, :] * product.reshape(vector.shape)


def reference(loads, dual_ops, precond, counts, signs):
    alive = live_slots(counts)
    signed = signs.astype(jnp.float32) * alive

    def assemble(contribution):
        return alive[..., None, :] * (contribution + neighbour_blocks(contribution))

    def inner(left, right):
        return 0.5 * jnp.sum(left * right, axis=(0, 1, 2, 4))

    residual = assemble(alive[..., None, :] * loads)
    multipliers = jnp.zeros_like(residual)
    direction = residual
    gamma_old = None
    for iteration in range(ITERS):
        smoothed = assemble(apply_local(precond, signed, residual))
        gamma_new = inner(residual, smoothed)
        if iteration == 0:
            direction = smoothed
        else:
            direction = smoothed + (gamma_new / gamma_old)[:, None] * direction
        image = assemble(apply_local(dual_ops, signed, direction))
        step_size = gamma_new / inner(direction, image)
        multipliers = multipliers + step_size[:, None] * direction
        residual = residual - step_size[:, None] * image
        gamma_old = gamma_new
    return multipliers, residual
```

```python
import jax
import jax.numpy as jnp
import numpy as np
from jax import lax
from jax.sharding import PartitionSpec as P

FACE = 96
EDGE = 16
ITERS = 2


DIRECTIONS = (
    (1, 0, 0),
    (-1, 0, 0),
    (0, 1, 0),
    (0, -1, 0),
    (0, 0, 1),
    (0, 0, -1),
    (1, 1, 0),
    (1, -1, 0),
    (-1, 1, 0),
    (-1, -1, 0),
    (1, 0, 1),
    (1, 0, -1),
    (-1, 0, 1),
    (-1, 0, -1),
    (0, 1, 1),
    (0, 1, -1),
    (0, -1, 1),
    (0, -1, -1),
)


def block_table():
    capacity = [FACE] * 6 + [EDGE] * 12
    offsets = [sum(capacity[:course]) for course in range(18)]
    return (capacity, offsets)


CAPACITY, OFFSETS = block_table()


def block(values, *heading):
    course = DIRECTIONS.index(heading)
    return values[:, OFFSETS[course] : OFFSETS[course] + CAPACITY[course]]


THIRD = 42


def pack(face, edge_a, edge_b, edge_c, edge_d, sums):
    top = jnp.concatenate([face, edge_a, edge_b], axis=1)
    rest = jnp.concatenate([edge_c, edge_d, *sums], axis=1)
    rest = jnp.pad(rest, ((0, 0), (0, THIRD - rest.shape[1])))
    low = jnp.concatenate([rest[0:4], rest[4:8], rest[8:12]], axis=1)
    low = jnp.pad(low, ((0, 0), (0, 128 - 3 * THIRD)))
    return jnp.concatenate([top, low], axis=0)


def unfold(low):
    return jnp.concatenate([low[:, THIRD * i : THIRD * (i + 1)] for i in range(3)], axis=0)


def unpack(tile):
    rest = unfold(tile[12:16])
    return (
        tile[:12, :FACE],
        tile[:12, FACE : FACE + EDGE],
        tile[:12, FACE + EDGE : FACE + 2 * EDGE],
        rest[:, :EDGE],
        rest[:, EDGE : 2 * EDGE],
    )


def shift_swap(axis, ahead, behind):
    ends = lax.axis_size(axis) - 1
    before = lax.ppermute(ahead, axis, [(i, i + 1) for i in range(ends)])
    after = lax.ppermute(behind, axis, [(i + 1, i) for i in range(ends)])
    return before, after


def pair_swap(axis, ahead, behind):
    count = lax.axis_size(axis)
    even = lax.axis_index(axis) % 2 == 0
    inner = [(i, i ^ 1) for i in range(count)]
    outer = [(i, i + 1 if i % 2 else i - 1) for i in range(1, count - 1)]
    near = lax.ppermute(jnp.where(even, ahead, behind), axis, inner)
    far = lax.ppermute(jnp.where(even, behind, ahead), axis, outer)
    return jnp.where(even, far, near), jnp.where(even, near, far)


def line_swap(axis, ahead, behind):
    count = lax.axis_size(axis)
    place = lax.axis_index(axis)
    target = lax.broadcasted_iota(jnp.int32, (count, 1, 1), 0)
    sent = jnp.where(target > place, ahead[None], behind[None])
    got = lax.all_to_all(sent, axis, 0, 0, tiled=True)
    before = lax.dynamic_index_in_dim(got, jnp.maximum(place - 1, 0), 0, keepdims=False)
    after = lax.dynamic_index_in_dim(got, jnp.minimum(place + 1, count - 1), 0, keepdims=False)
    return before, after, jnp.sum(got[:, 12:16, :], axis=0)


def exchange(y, sums=()):
    swaps = (shift_swap, shift_swap, pair_swap)

    def swap(stage, axis, ahead, behind):
        nonlocal sums
        ahead = pack(*ahead, sums)
        behind = pack(*behind, sums)
        if not sums:
            before, after = swaps[stage](axis, ahead, behind)
        else:
            before, after, low = line_swap(axis, ahead, behind)
            rest = unfold(low)
            sums = [rest[:, 2 * EDGE + i : 2 * EDGE + i + 1] for i in range(len(sums))]
        return unpack(before), unpack(after)

    mx, px = swap(
        0,
        "gx",
        (block(y, 1, 0, 0), block(y, 1, 1, 0), block(y, 1, -1, 0), block(y, 1, 0, 1), block(y, 1, 0, -1)),
        (block(y, -1, 0, 0), block(y, -1, 1, 0), block(y, -1, -1, 0), block(y, -1, 0, 1), block(y, -1, 0, -1)),
    )
    my, py = swap(
        1,
        "gy",
        (block(y, 0, 1, 0), mx[1], px[1], block(y, 0, 1, 1), block(y, 0, 1, -1)),
        (block(y, 0, -1, 0), mx[2], px[2], block(y, 0, -1, 1), block(y, 0, -1, -1)),
    )
    mz, pz = swap(
        2,
        "gz",
        (block(y, 0, 0, 1), mx[3], px[3], my[3], py[3]),
        (block(y, 0, 0, -1), mx[4], px[4], my[4], py[4]),
    )
    pieces = [
        px[0], mx[0], py[0], my[0], pz[0], mz[0],
        py[2], my[2], py[1], my[1],
        pz[2], mz[2], pz[1], mz[1],
        pz[4], mz[4], pz[3], mz[3],
    ]
    return jnp.concatenate(pieces, axis=1), sums


def per_device(loads, dual_ops, precond, counts, signs):
    order_max = sum(CAPACITY)
    owners = np.zeros((18, order_max), np.int32)
    position = np.zeros((order_max,), np.int32)
    for course in range(18):
        owners[course, OFFSETS[course] : OFFSETS[course] + CAPACITY[course]] = 1
        position[OFFSETS[course] : OFFSETS[course] + CAPACITY[course]] = np.arange(CAPACITY[course])
    limits = jnp.sum(counts[0, 0, 0][:, None] * jnp.asarray(owners, jnp.int32), axis=0)
    alive = (jnp.asarray(position, jnp.int32) < limits).astype(jnp.float32)
    signed = signs[0, 0, 0].astype(jnp.float32) * alive

    def local(matrix, vector):
        scaled = (signed * vector).astype(jnp.bfloat16)
        return signed * jnp.dot(scaled, matrix, preferred_element_type=jnp.float32)

    def dot(left, right):
        return jnp.sum(left * right, axis=1, keepdims=True)

    def assemble(contribution, sums=()):
        beside, sums = exchange(contribution, sums)
        return alive * (contribution + beside), sums

    dual_matrix = dual_ops[0, 0, 0]
    pre_matrix = precond[0, 0, 0]
    residual, _ = assemble(alive * loads[0, 0, 0])
    part = local(pre_matrix, residual)
    gamma_part = dot(residual, part)
    direction, _ = assemble(part)
    part = local(dual_matrix, direction)
    image, (gamma, curvature) = assemble(part, (gamma_part, dot(direction, part)))
    step = gamma / curvature
    multipliers = step * direction
    residual = residual - step * image
    for _ in range(1, ITERS):
        gamma_old = gamma
        part = local(pre_matrix, residual)
        smoothed, (gamma,) = assemble(part, (dot(residual, part),))
        direction = smoothed + (gamma / gamma_old) * direction
        part = local(dual_matrix, direction)
        image, (curvature,) = assemble(part, (dot(direction, part),))
        step = gamma / curvature
        multipliers = multipliers + step * direction
        residual = residual - step * image
    return (multipliers[None, None, None], residual[None, None, None])


def solution(mesh):
    placed = (
        P("gx", "gy", "gz", None, None),
        P("gx", "gy", "gz", None, None),
        P("gx", "gy", "gz", None, None),
        P("gx", "gy", "gz", None),
        P("gx", "gy", "gz", None),
    )
    return jax.shard_map(
        per_device,
        mesh=mesh,
        in_specs=placed,
        out_specs=(P("gx", "gy", "gz", None, None), P("gx", "gy", "gz", None, None)),
        check_vma=False,
    )
```

```python
import jax
import jax.numpy as jnp
import numpy as np
from jax import lax
from jax.sharding import PartitionSpec as P

FACE = 96
EDGE = 16
ITERS = 2


DIRECTIONS = (
    (1, 0, 0),
    (-1, 0, 0),
    (0, 1, 0),
    (0, -1, 0),
    (0, 0, 1),
    (0, 0, -1),
    (1, 1, 0),
    (1, -1, 0),
    (-1, 1, 0),
    (-1, -1, 0),
    (1, 0, 1),
    (1, 0, -1),
    (-1, 0, 1),
    (-1, 0, -1),
    (0, 1, 1),
    (0, 1, -1),
    (0, -1, 1),
    (0, -1, -1),
)


def block_table():
    capacity = [FACE] * 6 + [EDGE] * 12
    offsets = [sum(capacity[:course]) for course in range(18)]
    return (capacity, offsets)


CAPACITY, OFFSETS = block_table()


def block(values, *heading):
    course = DIRECTIONS.index(heading)
    return values[:, OFFSETS[course] : OFFSETS[course] + CAPACITY[course]]


THIRD = 42


def pack(face, edge_a, edge_b, edge_c, edge_d, sums):
    top = jnp.concatenate([face, edge_a, edge_b], axis=1)
    rest = jnp.concatenate([edge_c, edge_d, *sums], axis=1)
    rest = jnp.pad(rest, ((0, 0), (0, THIRD - rest.shape[1])))
    low = jnp.concatenate([rest[0:4], rest[4:8], rest[8:12]], axis=1)
    low = jnp.pad(low, ((0, 0), (0, 128 - 3 * THIRD)))
    return jnp.concatenate([top, low], axis=0)


def unfold(low):
    return jnp.concatenate([low[:, THIRD * i : THIRD * (i + 1)] for i in range(3)], axis=0)


def unpack(tile):
    rest = unfold(tile[12:16])
    return (
        tile[:12, :FACE],
        tile[:12, FACE : FACE + EDGE],
        tile[:12, FACE + EDGE : FACE + 2 * EDGE],
        rest[:, :EDGE],
        rest[:, EDGE : 2 * EDGE],
    )


def shift_swap(axis, ahead, behind):
    ends = lax.axis_size(axis) - 1
    before = lax.ppermute(ahead, axis, [(i, i + 1) for i in range(ends)])
    after = lax.ppermute(behind, axis, [(i + 1, i) for i in range(ends)])
    return before, after


def pair_swap(axis, ahead, behind):
    count = lax.axis_size(axis)
    even = lax.axis_index(axis) % 2 == 0
    inner = [(i, i ^ 1) for i in range(count)]
    outer = [(i, i + 1 if i % 2 else i - 1) for i in range(1, count - 1)]
    near = lax.ppermute(jnp.where(even, ahead, behind), axis, inner)
    far = lax.ppermute(jnp.where(even, behind, ahead), axis, outer)
    return jnp.where(even, far, near), jnp.where(even, near, far)


def line_swap(axis, ahead, behind, live):
    count = lax.axis_size(axis)
    later, index_before, index_after = live["place"][axis]
    sent = jnp.where(later, ahead[None], behind[None])
    sent, live = lax.optimization_barrier((sent, live))
    got = lax.all_to_all(sent, axis, 0, 0, tiled=True)
    got, live = lax.optimization_barrier((got, live))
    later, index_before, index_after = live["place"][axis]
    before = lax.dynamic_index_in_dim(got, index_before, 0, keepdims=False)
    after = lax.dynamic_index_in_dim(got, index_after, 0, keepdims=False)
    low = jnp.sum(got[:, 12:16, :], axis=0)
    before, after = lax.optimization_barrier((before, after))
    return before, after, low, live


def places():
    found = {}
    for axis in ("gx", "gy", "gz"):
        count = lax.axis_size(axis)
        place = lax.axis_index(axis)
        target = lax.broadcasted_iota(jnp.int32, (count, 16, 128), 0)
        found[axis] = (target > place, jnp.maximum(place - 1, 0), jnp.minimum(place + 1, count - 1))
    return found


def exchange(y, sums, live):
    swaps = (shift_swap, shift_swap, pair_swap)
    live = dict(live, y=y)

    def swap(stage, axis, ahead, behind):
        nonlocal sums, live
        ahead = pack(*ahead, sums)
        behind = pack(*behind, sums)
        if not sums:
            before, after = swaps[stage](axis, ahead, behind)
        else:
            before, after, low, live = line_swap(axis, ahead, behind, live)
            rest = unfold(low)
            sums = [rest[:, 2 * EDGE + i : 2 * EDGE + i + 1] for i in range(len(sums))]
        live = dict(live, **{axis: (before, after)})

    def from_neighbours(axis):
        return [unpack(tile) for tile in live[axis]]

    y = live["y"]
    swap(
        0,
        "gx",
        (block(y, 1, 0, 0), block(y, 1, 1, 0), block(y, 1, -1, 0), block(y, 1, 0, 1), block(y, 1, 0, -1)),
        (block(y, -1, 0, 0), block(y, -1, 1, 0), block(y, -1, -1, 0), block(y, -1, 0, 1), block(y, -1, 0, -1)),
    )
    y = live["y"]
    mx, px = from_neighbours("gx")
    swap(
        1,
        "gy",
        (block(y, 0, 1, 0), mx[1], px[1], block(y, 0, 1, 1), block(y, 0, 1, -1)),
        (block(y, 0, -1, 0), mx[2], px[2], block(y, 0, -1, 1), block(y, 0, -1, -1)),
    )
    y = live["y"]
    mx, px = from_neighbours("gx")
    my, py = from_neighbours("gy")
    swap(
        2,
        "gz",
        (block(y, 0, 0, 1), mx[3], px[3], my[3], py[3]),
        (block(y, 0, 0, -1), mx[4], px[4], my[4], py[4]),
    )
    mx, px = from_neighbours("gx")
    my, py = from_neighbours("gy")
    mz, pz = from_neighbours("gz")
    pieces = [
        px[0], mx[0], py[0], my[0], pz[0], mz[0],
        py[2], my[2], py[1], my[1],
        pz[2], mz[2], pz[1], mz[1],
        pz[4], mz[4], pz[3], mz[3],
    ]
    return live["y"] + jnp.concatenate(pieces, axis=1), sums, live


def per_device(loads, dual_ops, precond, counts, signs):
    order_max = sum(CAPACITY)
    owners = np.zeros((18, order_max), np.int32)
    position = np.zeros((order_max,), np.int32)
    for course in range(18):
        owners[course, OFFSETS[course] : OFFSETS[course] + CAPACITY[course]] = 1
        position[OFFSETS[course] : OFFSETS[course] + CAPACITY[course]] = np.arange(CAPACITY[course])
    limits = jnp.sum(counts[0, 0, 0][:, None] * jnp.asarray(owners, jnp.int32), axis=0)
    alive = (jnp.asarray(position, jnp.int32) < limits).astype(jnp.float32)
    signed = signs[0, 0, 0].astype(jnp.float32) * alive

    def dot(left, right):
        return jnp.sum(left * right, axis=1, keepdims=True)

    live = {"place": places(), "alive": alive, "signed": signed}
    live["dual"] = dual_ops[0, 0, 0]
    live["pre"] = precond[0, 0, 0]

    def assemble(contribution, sums=()):
        nonlocal live
        whole, sums, live = exchange(contribution, sums, live)
        return live["alive"] * whole, sums

    def local(name, vector):
        signed = live["signed"]
        scaled = (signed * vector).astype(jnp.bfloat16)
        return signed * jnp.dot(scaled, live[name], preferred_element_type=jnp.float32)

    live["residual"], _ = assemble(loads[0, 0, 0])
    part = local("pre", live["residual"])
    gamma_part = dot(live["residual"], part)
    live["direction"], _ = assemble(part)
    part = local("dual", live["direction"])
    image, (gamma, curvature) = assemble(part, (gamma_part, dot(live["direction"], part)))
    step = gamma / curvature
    live["multipliers"] = step * live["direction"]
    live["residual"] = live["residual"] - step * image
    live["gamma"] = gamma
    for _ in range(1, ITERS):
        part = local("pre", live["residual"])
        smoothed, (gamma,) = assemble(part, (dot(live["residual"], part),))
        live["direction"] = smoothed + (gamma / live["gamma"]) * live["direction"]
        live["gamma"] = gamma
        part = local("dual", live["direction"])
        image, (curvature,) = assemble(part, (dot(live["direction"], part),))
        step = live["gamma"] / curvature
        live["multipliers"] = live["multipliers"] + step * live["direction"]
        live["residual"] = live["residual"] - step * image
    multipliers, residual = live["multipliers"], live["residual"]
    return (multipliers[None, None, None], residual[None, None, None])


def solution(mesh):
    placed = (
        P("gx", "gy", "gz", None, None),
        P("gx", "gy", "gz", None, None),
        P("gx", "gy", "gz", None, None),
        P("gx", "gy", "gz", None),
        P("gx", "gy", "gz", None),
    )
    return jax.shard_map(
        per_device,
        mesh=mesh,
        in_specs=placed,
        out_specs=(P("gx", "gy", "gz", None, None), P("gx", "gy", "gz", None, None)),
        check_vma=False,
    )
```

```python
import jax
import jax.numpy as jnp
import numpy as np
from jax import lax
from jax.experimental import pallas as pl
from jax.experimental.pallas import tpu as pltpu
from jax.sharding import PartitionSpec as P

FACE = 96
EDGE = 16
ITERS = 2


DIRECTIONS = (
    (1, 0, 0),
    (-1, 0, 0),
    (0, 1, 0),
    (0, -1, 0),
    (0, 0, 1),
    (0, 0, -1),
    (1, 1, 0),
    (1, -1, 0),
    (-1, 1, 0),
    (-1, -1, 0),
    (1, 0, 1),
    (1, 0, -1),
    (-1, 0, 1),
    (-1, 0, -1),
    (0, 1, 1),
    (0, 1, -1),
    (0, -1, 1),
    (0, -1, -1),
)


def block_table():
    capacity = [FACE] * 6 + [EDGE] * 12
    offsets = [sum(capacity[:course]) for course in range(18)]
    return (capacity, offsets)


CAPACITY, OFFSETS = block_table()


def block(values, *heading):
    course = DIRECTIONS.index(heading)
    return values[:, OFFSETS[course] : OFFSETS[course] + CAPACITY[course]]


THIRD = 42


def pack(face, edge_a, edge_b, edge_c, edge_d, sums):
    top = jnp.concatenate([face, edge_a, edge_b], axis=1)
    rest = jnp.concatenate([edge_c, edge_d, *sums], axis=1)
    rest = jnp.pad(rest, ((0, 0), (0, THIRD - rest.shape[1])))
    low = jnp.concatenate([rest[0:4], rest[4:8], rest[8:12]], axis=1)
    low = jnp.pad(low, ((0, 0), (0, 128 - 3 * THIRD)))
    return jnp.concatenate([top, low], axis=0)


def unfold(low):
    return jnp.concatenate([low[:, THIRD * i : THIRD * (i + 1)] for i in range(3)], axis=0)


def unpack(tile):
    rest = unfold(tile[12:16])
    return (
        tile[:12, :FACE],
        tile[:12, FACE : FACE + EDGE],
        tile[:12, FACE + EDGE : FACE + 2 * EDGE],
        rest[:, :EDGE],
        rest[:, EDGE : 2 * EDGE],
    )


def messages(stage, y, mx, px, my, py, sums):
    if stage == 0:
        ahead = (block(y, 1, 0, 0), block(y, 1, 1, 0), block(y, 1, -1, 0), block(y, 1, 0, 1), block(y, 1, 0, -1))
        behind = (block(y, -1, 0, 0), block(y, -1, 1, 0), block(y, -1, -1, 0), block(y, -1, 0, 1), block(y, -1, 0, -1))
    elif stage == 1:
        ahead = (block(y, 0, 1, 0), mx[1], px[1], block(y, 0, 1, 1), block(y, 0, 1, -1))
        behind = (block(y, 0, -1, 0), mx[2], px[2], block(y, 0, -1, 1), block(y, 0, -1, -1))
    else:
        ahead = (block(y, 0, 0, 1), mx[3], px[3], my[3], py[3])
        behind = (block(y, 0, 0, -1), mx[4], px[4], my[4], py[4])
    return pack(*ahead, sums), pack(*behind, sums)


def beside(mx, px, my, py, mz, pz):
    pieces = [
        px[0], mx[0], py[0], my[0], pz[0], mz[0],
        py[2], my[2], py[1], my[1],
        pz[2], mz[2], pz[1], mz[1],
        pz[4], mz[4], pz[3], mz[3],
    ]
    return jnp.concatenate(pieces, axis=1)


AXES = ("gx", "gy", "gz")
TILE = jax.ShapeDtypeStruct((2, 16, 128), jnp.float32)


class Here:
    def __getitem__(self, stage):
        return lax.axis_index(AXES[stage])


HERE = Here()


def kernel_call(name, body, shapes, *operands, last=False):
    arrays = [pltpu.with_memory_space_constraint(value, pltpu.VMEM) for value in operands if value is not HERE]

    def kernel(*refs):
        given = iter(refs)
        results = body(*[HERE if value is HERE else next(given) for value in operands])
        for ref, result in zip(given, results):
            if isinstance(result, list):
                for i, part in enumerate(result):
                    ref[i] = part
            elif result.shape != ref.shape:
                lines = result.shape[1] // 128
                for i in range(lines):
                    ref[pl.ds(i, result.shape[0], stride=lines), :] = result[:, 128 * i : 128 * (i + 1)]
            else:
                ref[...] = result

    return pl.pallas_call(
        kernel,
        name=name,
        in_specs=[pl.BlockSpec(memory_space=pltpu.VMEM) for _ in arrays],
        out_specs=[pl.BlockSpec(memory_space=pltpu.VMEM) for _ in shapes],
        out_shape=[shape if last else pltpu.VMEM(shape.shape, shape.dtype) for shape in shapes],
    )(*arrays)


def spread(ahead, behind, place, count):
    return [jnp.where(place < i, ahead, behind) for i in range(count)]


def pair_of(tiles):
    return unpack(tiles[0]), unpack(tiles[1])


def permuted(axis, tiles, place):
    count = lax.axis_size(axis)
    if axis != "gz":
        before = lax.ppermute(tiles[0], axis, [(i, i + 1) for i in range(count - 1)])
        after = lax.ppermute(tiles[1], axis, [(i + 1, i) for i in range(count - 1)])
        return before, after
    near = lax.ppermute(tiles[0], axis, [(i, i ^ 1) for i in range(count)])
    far = lax.ppermute(tiles[1], axis, [(i, i + 1 if i % 2 else i - 1) for i in range(1, count - 1)])
    return near, far


def exchange_by_permutes(y, sent, place):
    tile = jax.ShapeDtypeStruct((16, 128), jnp.float32)
    x_tiles = permuted("gx", sent, place)

    def second(y, mx, px, place):
        return messages(1, y[...], unpack(mx[...]), unpack(px[...]), None, None, ())

    sent = kernel_call("second", second, (tile, tile), y, *x_tiles, place)
    y_tiles = permuted("gy", sent, place)

    def third(y, mx, px, my, py, place):
        ahead, behind = messages(2, y[...], *[unpack(v[...]) for v in (mx, px, my, py)], ())
        even = lax.rem(place[2], 2) == 0
        return jnp.where(even, ahead, behind), jnp.where(even, behind, ahead)

    sent = kernel_call("third", third, (tile, tile), y, *x_tiles, *y_tiles, place)
    return (*x_tiles, *y_tiles, *permuted("gz", sent, place))


def from_permutes(tiles, place):
    mx, px, my, py, near, far = [value[...] for value in tiles]
    even = lax.rem(place[2], 2) == 0
    mz, pz = jnp.where(even, far, near), jnp.where(even, near, far)
    return beside(*[unpack(value) for value in (mx, px, my, py, mz, pz)])


def gathered(stage, axis, sent, live):
    sent, live = lax.optimization_barrier((sent, live))
    got = lax.all_to_all(sent, axis, 0, 0, tiled=True)
    return lax.optimization_barrier((got, live))


def picked(got, place, stage, number):
    count = got.shape[0]
    here = place[stage]
    before = got[jnp.maximum(here - 1, 0)]
    after = got[jnp.minimum(here + 1, count - 1)]
    low = got[0, 12:16, :]
    for i in range(1, count):
        low = low + got[i, 12:16, :]
    rest = unfold(low)
    return before, after, [rest[:, 2 * EDGE + i : 2 * EDGE + i + 1] for i in range(number)]


def exchange_by_gathers(y, sent, place, number, live):
    sizes = [lax.axis_size(axis) for axis in AXES]

    def blocks(stage):
        return jax.ShapeDtypeStruct((sizes[stage], 16, 128), jnp.float32)

    live = dict(live, y=y)
    got, live = gathered(0, "gx", sent, live)

    def second(y, got, place):
        before, after, sums = picked(got, place, 0, number)
        ahead, behind = messages(1, y[...], unpack(before), unpack(after), None, None, sums)
        return spread(ahead, behind, place[1], sizes[1]), [before, after]

    sent, x_tiles = kernel_call("second_sum", second, (blocks(1), TILE), live["y"], got, HERE)
    live["x_tiles"] = x_tiles
    got, live = gathered(1, "gy", sent, live)

    def third(y, x_tiles, got, place):
        before, after, sums = picked(got, place, 1, number)
        ahead, behind = messages(2, y[...], *pair_of(x_tiles), unpack(before), unpack(after), sums)
        return spread(ahead, behind, place[2], sizes[2]), [before, after]

    sent, y_tiles = kernel_call("third_sum", third, (blocks(2), TILE), live["y"], live["x_tiles"], got, HERE)
    live["y_tiles"] = y_tiles
    return gathered(2, "gz", sent, live)


def from_gathers(got, x_tiles, y_tiles, place, number):
    before, after, sums = picked(got, place, 2, number)
    return beside(*pair_of(x_tiles), *pair_of(y_tiles), unpack(before), unpack(after)), sums


def per_device(loads, dual_ops, precond, counts, signs):
    order_max = sum(CAPACITY)
    owners = np.zeros((18, order_max), np.int32)
    position = np.zeros((order_max,), np.int32)
    for course in range(18):
        owners[course, OFFSETS[course] : OFFSETS[course] + CAPACITY[course]] = 1
        position[OFFSETS[course] : OFFSETS[course] + CAPACITY[course]] = np.arange(CAPACITY[course])
    limits = jnp.sum(counts[0, 0, 0][:, None] * jnp.asarray(owners, jnp.int32), axis=0)
    alive = (jnp.asarray(position, jnp.int32) < limits).astype(jnp.float32)[None]
    signed = signs[0, 0, 0].astype(jnp.float32)[None] * alive
    place = HERE
    dual, pre = dual_ops[0, 0, 0], precond[0, 0, 0]
    loads = loads[0, 0, 0]
    sizes = [lax.axis_size(axis) for axis in AXES]
    vector = jax.ShapeDtypeStruct(loads.shape, jnp.float32)
    rounded = jax.ShapeDtypeStruct(loads.shape, jnp.bfloat16)
    column = jax.ShapeDtypeStruct((loads.shape[0], 1), jnp.float32)
    tile = jax.ShapeDtypeStruct((16, 128), jnp.float32)
    first_blocks = jax.ShapeDtypeStruct((sizes[0], 16, 128), jnp.float32)

    def times(scaled, matrix):
        return jnp.dot(scaled, matrix, preferred_element_type=jnp.float32)

    def dot(left, right):
        return jnp.sum(left * right, axis=1, keepdims=True)

    def load_tiles(loads, place):
        return messages(0, loads[...], None, None, None, None, ())

    sent = kernel_call("load_tiles", load_tiles, (tile, tile), loads, place)
    tiles = exchange_by_permutes(loads, sent, place)

    def begin(y, alive, signed, place, *tiles):
        residual = alive[...] * (y[...] + from_permutes(tiles, place))
        return residual, (signed[...] * residual).astype(jnp.bfloat16)

    residual, scaled = kernel_call("begin", begin, (vector, rounded), loads, alive, signed, place, *tiles)

    def precond_tiles(product, signed, residual, place):
        y = signed[...] * product[...]
        return (y, dot(residual[...], y), *messages(0, y, None, None, None, None, ()))

    y, gamma_part, *sent = kernel_call(
        "precond_tiles", precond_tiles, (vector, column, tile, tile), times(scaled, pre), signed, residual, place
    )
    tiles = exchange_by_permutes(y, sent, place)

    def aim(y, alive, signed, place, *tiles):
        direction = alive[...] * (y[...] + from_permutes(tiles, place))
        return direction, (signed[...] * direction).astype(jnp.bfloat16)

    direction, scaled = kernel_call("aim", aim, (vector, rounded), y, alive, signed, place, *tiles)

    live = dict(alive=alive, signed=signed, residual=residual, direction=direction, dual=dual, pre=pre)

    def image_blocks(product, signed, direction, gamma_part, place):
        y = signed[...] * product[...]
        sums = (gamma_part[...], dot(direction[...], y))
        return y, spread(*messages(0, y, None, None, None, None, sums), place[0], sizes[0])

    y, sent = kernel_call(
        "image_blocks",
        image_blocks,
        (vector, first_blocks),
        times(scaled, live["dual"]),
        signed,
        direction,
        gamma_part,
        place,
    )
    got, live = exchange_by_gathers(y, sent, place, 2, live)

    def first_step(got, x_tiles, y_tiles, y, place, alive, signed, direction, residual):
        near, (gamma, curvature) = from_gathers(got, x_tiles, y_tiles, place, 2)
        image = alive[...] * (y[...] + near)
        step = gamma / curvature
        left = residual[...] - step * image
        return step * direction[...], left, (signed[...] * left).astype(jnp.bfloat16), gamma

    names = ("x_tiles", "y_tiles", "y", "place", "alive", "signed", "direction", "residual")
    live["multipliers"], live["residual"], scaled, live["gamma"] = kernel_call(
        "first_step", first_step, (vector, vector, rounded, column), got, *[live[name] if name != "place" else HERE for name in names]
    )

    def sum_blocks(product, signed, left, place):
        y = signed[...] * product[...]
        sums = (dot(left[...], y),)
        return y, spread(*messages(0, y, None, None, None, None, sums), place[0], sizes[0])

    for iteration in range(1, ITERS):
        y, sent = kernel_call(
            "smooth_blocks",
            sum_blocks,
            (vector, first_blocks),
            times(scaled, live["pre"]),
            live["signed"],
            live["residual"],
            HERE,
        )
        got, live = exchange_by_gathers(y, sent, HERE, 1, live)

        def turn(got, x_tiles, y_tiles, y, place, alive, signed, direction, gamma_old):
            near, (gamma,) = from_gathers(got, x_tiles, y_tiles, place, 1)
            smoothed = alive[...] * (y[...] + near)
            turned = smoothed + (gamma / gamma_old[...]) * direction[...]
            return turned, (signed[...] * turned).astype(jnp.bfloat16), gamma

        names = ("x_tiles", "y_tiles", "y", "place", "alive", "signed", "direction", "gamma")
        live["direction"], scaled, live["gamma"] = kernel_call(
            "turn", turn, (vector, rounded, column), got, *[live[name] if name != "place" else HERE for name in names]
        )
        y, sent = kernel_call(
            "sum_blocks",
            sum_blocks,
            (vector, first_blocks),
            times(scaled, live["dual"]),
            live["signed"],
            live["direction"],
            HERE,
        )
        got, live = exchange_by_gathers(y, sent, HERE, 1, live)

        def advance(got, x_tiles, y_tiles, y, place, alive, signed, direction, gamma, multipliers, residual):
            near, (curvature,) = from_gathers(got, x_tiles, y_tiles, place, 1)
            image = alive[...] * (y[...] + near)
            step = gamma[...] / curvature
            left = residual[...] - step * image
            results = (multipliers[...] + step * direction[...], left)
            if iteration < ITERS - 1:
                results += ((signed[...] * left).astype(jnp.bfloat16),)
            return results

        lines = jax.ShapeDtypeStruct((loads.size // 128, 128), jnp.float32)
        shapes = (vector, vector, rounded) if iteration < ITERS - 1 else (lines, lines)
        names = ("x_tiles", "y_tiles", "y", "place", "alive", "signed", "direction", "gamma", "multipliers", "residual")
        live["multipliers"], live["residual"], *rest = kernel_call(
            "advance",
            advance,
            shapes,
            got,
            *[live[name] if name != "place" else HERE for name in names],
            last=iteration == ITERS - 1,
        )
        if rest:
            scaled = rest[0]
    whole = (1, 1, 1, *loads.shape)
    return (live["multipliers"].reshape(whole), live["residual"].reshape(whole))


def solution(mesh):
    placed = (
        P("gx", "gy", "gz", None, None),
        P("gx", "gy", "gz", None, None),
        P("gx", "gy", "gz", None, None),
        P("gx", "gy", "gz", None),
        P("gx", "gy", "gz", None),
    )
    return jax.shard_map(
        per_device,
        mesh=mesh,
        in_specs=placed,
        out_specs=(P("gx", "gy", "gz", None, None), P("gx", "gy", "gz", None, None)),
        check_vma=False,
    )
```

```python
import jax
import jax.numpy as jnp
import numpy as np
from jax import lax
from jax.experimental import pallas as pl
from jax.experimental.pallas import tpu as pltpu
from jax.sharding import PartitionSpec as P

FACE = 96
EDGE = 16
ITERS = 2


DIRECTIONS = (
    (1, 0, 0),
    (-1, 0, 0),
    (0, 1, 0),
    (0, -1, 0),
    (0, 0, 1),
    (0, 0, -1),
    (1, 1, 0),
    (1, -1, 0),
    (-1, 1, 0),
    (-1, -1, 0),
    (1, 0, 1),
    (1, 0, -1),
    (-1, 0, 1),
    (-1, 0, -1),
    (0, 1, 1),
    (0, 1, -1),
    (0, -1, 1),
    (0, -1, -1),
)


def block_table():
    capacity = [FACE] * 6 + [EDGE] * 12
    offsets = [sum(capacity[:course]) for course in range(18)]
    return (capacity, offsets)


CAPACITY, OFFSETS = block_table()


def block(values, *heading):
    course = DIRECTIONS.index(heading)
    return values[:, OFFSETS[course] : OFFSETS[course] + CAPACITY[course]]


THIRD = 42


def pack(face, edge_a, edge_b, edge_c, edge_d, sums):
    top = jnp.concatenate([face, edge_a, edge_b], axis=1)
    rest = jnp.concatenate([edge_c, edge_d, *sums], axis=1)
    rest = jnp.pad(rest, ((0, 0), (0, THIRD - rest.shape[1])))
    low = jnp.concatenate([rest[0:4], rest[4:8], rest[8:12]], axis=1)
    low = jnp.pad(low, ((0, 0), (0, 128 - 3 * THIRD)))
    return jnp.concatenate([top, low], axis=0)


def unfold(low):
    return jnp.concatenate([low[:, THIRD * i : THIRD * (i + 1)] for i in range(3)], axis=0)


def unpack(tile):
    rest = unfold(tile[12:16])
    return (
        tile[:12, :FACE],
        tile[:12, FACE : FACE + EDGE],
        tile[:12, FACE + EDGE : FACE + 2 * EDGE],
        rest[:, :EDGE],
        rest[:, EDGE : 2 * EDGE],
    )


def messages(stage, y, mx, px, my, py, sums):
    if stage == 0:
        ahead = (block(y, 1, 0, 0), block(y, 1, 1, 0), block(y, 1, -1, 0), block(y, 1, 0, 1), block(y, 1, 0, -1))
        behind = (block(y, -1, 0, 0), block(y, -1, 1, 0), block(y, -1, -1, 0), block(y, -1, 0, 1), block(y, -1, 0, -1))
    elif stage == 1:
        ahead = (block(y, 0, 1, 0), mx[1], px[1], block(y, 0, 1, 1), block(y, 0, 1, -1))
        behind = (block(y, 0, -1, 0), mx[2], px[2], block(y, 0, -1, 1), block(y, 0, -1, -1))
    else:
        ahead = (block(y, 0, 0, 1), mx[3], px[3], my[3], py[3])
        behind = (block(y, 0, 0, -1), mx[4], px[4], my[4], py[4])
    return pack(*ahead, sums), pack(*behind, sums)


def beside(mx, px, my, py, mz, pz):
    pieces = [
        px[0], mx[0], py[0], my[0], pz[0], mz[0],
        py[2], my[2], py[1], my[1],
        pz[2], mz[2], pz[1], mz[1],
        pz[4], mz[4], pz[3], mz[3],
    ]
    return jnp.concatenate(pieces, axis=1)


AXES = ("gx", "gy", "gz")
TILE = jax.ShapeDtypeStruct((2, 16, 128), jnp.float32)


class Here:
    def __getitem__(self, stage):
        return lax.axis_index(AXES[stage])


HERE = Here()


def kernel_call(name, body, shapes, *operands, last=False):
    arrays = [pltpu.with_memory_space_constraint(value, pltpu.VMEM) for value in operands if value is not HERE]

    def kernel(*refs):
        given = iter(refs)
        results = body(*[HERE if value is HERE else next(given) for value in operands])
        for ref, result in zip(given, results):
            if isinstance(result, list):
                for i, part in enumerate(result):
                    at, part = part if isinstance(part, tuple) else (i, part)
                    if part is None or part.shape != ref.shape[1:]:
                        ref[at] = jnp.zeros(ref.shape[1:], ref.dtype)
                    if part is not None:
                        ref[at, : part.shape[0], : part.shape[1]] = part
            elif result.shape != ref.shape:
                lines = result.shape[1] // 128
                for i in range(lines):
                    ref[pl.ds(i, result.shape[0], stride=lines), :] = result[:, 128 * i : 128 * (i + 1)]
            else:
                ref[...] = result

    return pl.pallas_call(
        kernel,
        name=name,
        in_specs=[pl.BlockSpec(memory_space=pltpu.VMEM) for _ in arrays],
        out_specs=[pl.BlockSpec(memory_space=pltpu.VMEM) for _ in shapes],
        out_shape=[shape if last else pltpu.VMEM(shape.shape, shape.dtype) for shape in shapes],
    )(*arrays)


def spread(ahead, behind, place, count):
    return [jnp.where(place < i, ahead, behind) for i in range(count)]


def pair_of(tiles):
    return unpack(tiles[0]), unpack(tiles[1])


MASK = (4, 2, 1)
PAIRS = ((0, 1), (0, 2), (1, 2))


def cubes(kind):
    sizes = [lax.axis_size(axis) for axis in AXES]
    found = {}
    for place in np.ndindex(*sizes):
        corner = tuple((i + kind) // 2 % (size // 2) for i, size in zip(place, sizes))
        member = sum(mask * (i % 2) for mask, i in zip(MASK, place))
        found.setdefault(corner, {})[member] = int(np.ravel_multi_index(place, sizes))
    return [[members[i] for i in range(8)] for members in found.values()]


def heading_of(signs_by_axis):
    return tuple(signs_by_axis.get(axis, 0) for axis in range(3))


class Parity:
    def __init__(self, place):
        parities = [lax.rem(place[axis], 2) for axis in range(3)]
        self.even = [value == 0 for value in parities]
        self.position = sum(mask * value for mask, value in zip(MASK, parities))

    def choose(self, axes, values):
        if len(axes) == 1:
            return jnp.where(self.even[axes[0]], values(0), values(1))
        return jnp.where(
            self.even[axes[0]],
            jnp.where(self.even[axes[1]], values(0, 0), values(0, 1)),
            jnp.where(self.even[axes[1]], values(1, 0), values(1, 1)),
        )

    def own(self, y, axes, kinds):
        def value(*odd):
            return block(y, *heading_of({axis: 1 - 2 * (kind ^ i) for axis, kind, i in zip(axes, kinds, odd)}))

        return self.choose(axes, value)

    def toward(self, axes, signs, by_kinds):
        return self.choose(axes, lambda *odd: by_kinds[tuple(sign ^ i for sign, i in zip(signs, odd))])


def cube_b(y, parity):
    sent = []
    for axis in range(3):
        rest = [other for other in range(3) if other != axis]
        parts = [parity.own(y, (axis,), (1,))]
        for other in rest:
            first, second = sorted((axis, other))
            parts.append(parity.own(y, (first, second), (int(first == axis), int(second == axis))))
        sent.append((MASK[axis], jnp.concatenate(parts, axis=1)))
    for pair in PAIRS:
        sent.append((MASK[pair[0]] | MASK[pair[1]], parity.own(y, pair, (1, 1))))
    return sent


def members(got, parity):
    return {mask: got[parity.position ^ mask][:12] for mask in range(1, 7)}


def edge_at(tile, number):
    return tile[:, FACE + EDGE * number : FACE + EDGE * (number + 1)]


def passed(axis, other):
    return [i for i in range(3) if i != axis].index(other)


def cube_a(y, parity, from_b):
    sent = []
    for axis in range(3):
        parts = [parity.own(y, (axis,), (0,))]
        for other in range(3):
            if other != axis:
                parts.append(edge_at(from_b[MASK[other]], passed(other, axis)))
        sent.append((MASK[axis], jnp.concatenate(parts, axis=1)))
    for pair in PAIRS:
        sent.append((MASK[pair[0]] | MASK[pair[1]], parity.own(y, pair, (0, 0))))
    return sent


def cube_beside(parity, from_a, from_b):
    faces, edges = {}, {}
    for axis in range(3):
        by_kinds = {(0,): from_a[MASK[axis]][:, :FACE], (1,): from_b[MASK[axis]][:, :FACE]}
        for sign in range(2):
            faces[heading_of({axis: 1 - 2 * sign})] = parity.toward((axis,), (sign,), by_kinds)
    for pair in PAIRS:
        mask = MASK[pair[0]] | MASK[pair[1]]
        first, second = pair
        by_kinds = {
            (0, 0): from_a[mask][:, :EDGE],
            (1, 1): from_b[mask][:, :EDGE],
            (0, 1): edge_at(from_a[MASK[first]], passed(first, second)),
            (1, 0): edge_at(from_a[MASK[second]], passed(second, first)),
        }
        for signs in np.ndindex(2, 2):
            heading = heading_of({axis: 1 - 2 * sign for axis, sign in zip(pair, signs)})
            edges[heading] = parity.toward(pair, signs, by_kinds)
    return jnp.concatenate([{**faces, **edges}[heading] for heading in DIRECTIONS], axis=1)


def placed(sent, parity):
    blocks = {mask: value for mask, value in sent}
    return [(parity.position ^ mask, blocks.get(mask)) for mask in range(8)]


def cube_swap(kind, sent, live):
    sent, live = lax.optimization_barrier((sent, live))
    got = lax.all_to_all(sent, AXES, 0, 0, axis_index_groups=cubes(kind), tiled=True)
    return lax.optimization_barrier((got, live))


CUBE = jax.ShapeDtypeStruct((8, 16, 128), jnp.float32)


def exchange_by_cubes(sent, live):
    got, live = cube_swap(1, sent, live)
    live["from_b"] = got

    def second(y, from_b):
        parity = Parity(HERE)
        return (placed(cube_a(y[...], parity, members(from_b, parity)), parity),)

    (sent,) = kernel_call("cube_a", second, (CUBE,), live["y"], live["from_b"])
    got, live = cube_swap(0, sent, live)
    live["from_a"] = got
    return live


def from_cubes(from_a, from_b):
    parity = Parity(HERE)
    return cube_beside(parity, members(from_a, parity), members(from_b, parity))


def gathered(stage, axis, sent, live):
    sent, live = lax.optimization_barrier((sent, live))
    got = lax.all_to_all(sent, axis, 0, 0, tiled=True)
    return lax.optimization_barrier((got, live))


def picked(got, place, stage, number):
    count = got.shape[0]
    here = place[stage]
    before = got[jnp.maximum(here - 1, 0)]
    after = got[jnp.minimum(here + 1, count - 1)]
    low = got[0, 12:16, :]
    for i in range(1, count):
        low = low + got[i, 12:16, :]
    rest = unfold(low)
    return before, after, [rest[:, 2 * EDGE + i : 2 * EDGE + i + 1] for i in range(number)]


def exchange_by_gathers(y, sent, place, number, live):
    sizes = [lax.axis_size(axis) for axis in AXES]

    def blocks(stage):
        return jax.ShapeDtypeStruct((sizes[stage], 16, 128), jnp.float32)

    live = dict(live, y=y)
    got, live = gathered(0, "gx", sent, live)

    def second(y, got, place):
        before, after, sums = picked(got, place, 0, number)
        ahead, behind = messages(1, y[...], unpack(before), unpack(after), None, None, sums)
        return spread(ahead, behind, place[1], sizes[1]), [before, after]

    sent, x_tiles = kernel_call("second_sum", second, (blocks(1), TILE), live["y"], got, HERE)
    live["x_tiles"] = x_tiles
    got, live = gathered(1, "gy", sent, live)

    def third(y, x_tiles, got, place):
        before, after, sums = picked(got, place, 1, number)
        ahead, behind = messages(2, y[...], *pair_of(x_tiles), unpack(before), unpack(after), sums)
        return spread(ahead, behind, place[2], sizes[2]), [before, after]

    sent, y_tiles = kernel_call("third_sum", third, (blocks(2), TILE), live["y"], live["x_tiles"], got, HERE)
    live["y_tiles"] = y_tiles
    return gathered(2, "gz", sent, live)


def from_gathers(got, x_tiles, y_tiles, place, number):
    before, after, sums = picked(got, place, 2, number)
    return beside(*pair_of(x_tiles), *pair_of(y_tiles), unpack(before), unpack(after)), sums


def per_device(loads, dual_ops, precond, counts, signs):
    place = HERE
    dual, pre = dual_ops[0, 0, 0], precond[0, 0, 0]
    loads = loads[0, 0, 0]
    sizes = [lax.axis_size(axis) for axis in AXES]
    vector = jax.ShapeDtypeStruct(loads.shape, jnp.float32)
    rounded = jax.ShapeDtypeStruct(loads.shape, jnp.bfloat16)
    column = jax.ShapeDtypeStruct((loads.shape[0], 1), jnp.float32)
    first_blocks = jax.ShapeDtypeStruct((sizes[0], 16, 128), jnp.float32)

    def times(scaled, matrix):
        return jnp.dot(scaled, matrix, preferred_element_type=jnp.float32)

    def dot(left, right):
        return jnp.sum(left * right, axis=1, keepdims=True)

    def load_blocks(loads, counts, signs):
        position = lax.broadcasted_iota(jnp.int32, (1, FACE), 1)
        alive = [
            (position[:, : CAPACITY[course]] < counts[:, course : course + 1]).astype(jnp.float32)
            for course in range(len(DIRECTIONS))
        ]
        alive = jnp.concatenate(alive, axis=1)
        parity = Parity(HERE)
        return alive, signs[...].astype(jnp.float32) * alive, placed(cube_b(loads[...], parity), parity)

    row = jax.ShapeDtypeStruct((1, loads.shape[1]), jnp.float32)
    live = dict(dual=dual, pre=pre)
    live["alive"], live["signed"], sent = kernel_call(
        "load_blocks", load_blocks, (row, row, CUBE), loads, counts[0, 0], signs[0, 0]
    )
    live["y"] = loads
    live = exchange_by_cubes(sent, live)

    def assemble(y, alive, signed, from_a, from_b):
        whole = alive[...] * (y[...] + from_cubes(from_a, from_b))
        return whole, (signed[...] * whole).astype(jnp.bfloat16)

    names = ("y", "alive", "signed", "from_a", "from_b")
    live["residual"], scaled = kernel_call("begin", assemble, (vector, rounded), *[live.pop(name) if name[0] in "fy" else live[name] for name in names])

    def precond_blocks(product, signed, residual):
        y = signed[...] * product[...]
        parity = Parity(HERE)
        return y, dot(residual[...], y), placed(cube_b(y, parity), parity)

    live["y"], live["gamma_part"], sent = kernel_call(
        "precond_blocks",
        precond_blocks,
        (vector, column, CUBE),
        times(scaled, live["pre"]),
        live["signed"],
        live["residual"],
    )
    live = exchange_by_cubes(sent, live)
    live["direction"], scaled = kernel_call("aim", assemble, (vector, rounded), *[live.pop(name) if name[0] in "fy" else live[name] for name in names])

    def image_blocks(product, signed, direction, gamma_part, place):
        y = signed[...] * product[...]
        sums = (gamma_part[...], dot(direction[...], y))
        return y, spread(*messages(0, y, None, None, None, None, sums), place[0], sizes[0])

    y, sent = kernel_call(
        "image_blocks",
        image_blocks,
        (vector, first_blocks),
        times(scaled, live["dual"]),
        live["signed"],
        live["direction"],
        live.pop("gamma_part"),
        place,
    )
    got, live = exchange_by_gathers(y, sent, place, 2, live)

    def first_step(got, x_tiles, y_tiles, y, place, alive, signed, direction, residual):
        near, (gamma, curvature) = from_gathers(got, x_tiles, y_tiles, place, 2)
        image = alive[...] * (y[...] + near)
        step = gamma / curvature
        left = residual[...] - step * image
        return step * direction[...], left, (signed[...] * left).astype(jnp.bfloat16), gamma

    names = ("x_tiles", "y_tiles", "y", "place", "alive", "signed", "direction", "residual")
    live["multipliers"], live["residual"], scaled, live["gamma"] = kernel_call(
        "first_step", first_step, (vector, vector, rounded, column), got, *[live[name] if name != "place" else HERE for name in names]
    )

    def sum_blocks(product, signed, left, place):
        y = signed[...] * product[...]
        sums = (dot(left[...], y),)
        return y, spread(*messages(0, y, None, None, None, None, sums), place[0], sizes[0])

    for iteration in range(1, ITERS):
        y, sent = kernel_call(
            "smooth_blocks",
            sum_blocks,
            (vector, first_blocks),
            times(scaled, live["pre"]),
            live["signed"],
            live["residual"],
            HERE,
        )
        got, live = exchange_by_gathers(y, sent, HERE, 1, live)

        def turn(got, x_tiles, y_tiles, y, place, alive, signed, direction, gamma_old):
            near, (gamma,) = from_gathers(got, x_tiles, y_tiles, place, 1)
            smoothed = alive[...] * (y[...] + near)
            turned = smoothed + (gamma / gamma_old[...]) * direction[...]
            return turned, (signed[...] * turned).astype(jnp.bfloat16), gamma

        names = ("x_tiles", "y_tiles", "y", "place", "alive", "signed", "direction", "gamma")
        live["direction"], scaled, live["gamma"] = kernel_call(
            "turn", turn, (vector, rounded, column), got, *[live[name] if name != "place" else HERE for name in names]
        )
        y, sent = kernel_call(
            "sum_blocks",
            sum_blocks,
            (vector, first_blocks),
            times(scaled, live["dual"]),
            live["signed"],
            live["direction"],
            HERE,
        )
        got, live = exchange_by_gathers(y, sent, HERE, 1, live)

        def advance(got, x_tiles, y_tiles, y, place, alive, signed, direction, gamma, multipliers, residual):
            near, (curvature,) = from_gathers(got, x_tiles, y_tiles, place, 1)
            image = alive[...] * (y[...] + near)
            step = gamma[...] / curvature
            left = residual[...] - step * image
            results = (multipliers[...] + step * direction[...], left)
            if iteration < ITERS - 1:
                results += ((signed[...] * left).astype(jnp.bfloat16),)
            return results

        lines = jax.ShapeDtypeStruct((loads.size // 128, 128), jnp.float32)
        shapes = (vector, vector, rounded) if iteration < ITERS - 1 else (lines, lines)
        names = ("x_tiles", "y_tiles", "y", "place", "alive", "signed", "direction", "gamma", "multipliers", "residual")
        live["multipliers"], live["residual"], *rest = kernel_call(
            "advance",
            advance,
            shapes,
            got,
            *[live[name] if name != "place" else HERE for name in names],
            last=iteration == ITERS - 1,
        )
        if rest:
            scaled = rest[0]
    whole = (1, 1, 1, *loads.shape)
    return (live["multipliers"].reshape(whole), live["residual"].reshape(whole))


def solution(mesh):
    placed = (
        P("gx", "gy", "gz", None, None),
        P("gx", "gy", "gz", None, None),
        P("gx", "gy", "gz", None, None),
        P("gx", "gy", "gz", None),
        P("gx", "gy", "gz", None),
    )
    return jax.shard_map(
        per_device,
        mesh=mesh,
        in_specs=placed,
        out_specs=(P("gx", "gy", "gz", None, None), P("gx", "gy", "gz", None, None)),
        check_vma=False,
    )
```

```python
import jax
import jax.numpy as jnp
import numpy as np
from jax import lax
from jax.experimental import pallas as pl
from jax.experimental.pallas import tpu as pltpu
from jax.sharding import PartitionSpec as P

FACE = 96
EDGE = 16
ITERS = 2


DIRECTIONS = (
    (1, 0, 0),
    (-1, 0, 0),
    (0, 1, 0),
    (0, -1, 0),
    (0, 0, 1),
    (0, 0, -1),
    (1, 1, 0),
    (1, -1, 0),
    (-1, 1, 0),
    (-1, -1, 0),
    (1, 0, 1),
    (1, 0, -1),
    (-1, 0, 1),
    (-1, 0, -1),
    (0, 1, 1),
    (0, 1, -1),
    (0, -1, 1),
    (0, -1, -1),
)


def block_table():
    capacity = [FACE] * 6 + [EDGE] * 12
    offsets = [sum(capacity[:course]) for course in range(18)]
    return (capacity, offsets)


CAPACITY, OFFSETS = block_table()


def block(values, *heading):
    course = DIRECTIONS.index(heading)
    return values[:, OFFSETS[course] : OFFSETS[course] + CAPACITY[course]]


THIRD = 42


def pack(face, edge_a, edge_b, edge_c, edge_d, sums):
    top = jnp.concatenate([face, edge_a, edge_b], axis=1)
    rest = jnp.concatenate([edge_c, edge_d, *sums], axis=1)
    rest = jnp.pad(rest, ((0, 0), (0, THIRD - rest.shape[1])))
    low = jnp.concatenate([rest[0:4], rest[4:8], rest[8:12]], axis=1)
    low = jnp.pad(low, ((0, 0), (0, 128 - 3 * THIRD)))
    return jnp.concatenate([top, low], axis=0)


def unfold(low):
    return jnp.concatenate([low[:, THIRD * i : THIRD * (i + 1)] for i in range(3)], axis=0)


def unpack(tile):
    rest = unfold(tile[12:16])
    return (
        tile[:12, :FACE],
        tile[:12, FACE : FACE + EDGE],
        tile[:12, FACE + EDGE : FACE + 2 * EDGE],
        rest[:, :EDGE],
        rest[:, EDGE : 2 * EDGE],
    )


def messages(stage, y, mx, px, my, py, sums):
    if stage == 0:
        ahead = (block(y, 1, 0, 0), block(y, 1, 1, 0), block(y, 1, -1, 0), block(y, 1, 0, 1), block(y, 1, 0, -1))
        behind = (block(y, -1, 0, 0), block(y, -1, 1, 0), block(y, -1, -1, 0), block(y, -1, 0, 1), block(y, -1, 0, -1))
    elif stage == 1:
        ahead = (block(y, 0, 1, 0), mx[1], px[1], block(y, 0, 1, 1), block(y, 0, 1, -1))
        behind = (block(y, 0, -1, 0), mx[2], px[2], block(y, 0, -1, 1), block(y, 0, -1, -1))
    else:
        ahead = (block(y, 0, 0, 1), mx[3], px[3], my[3], py[3])
        behind = (block(y, 0, 0, -1), mx[4], px[4], my[4], py[4])
    return pack(*ahead, sums), pack(*behind, sums)


def beside(mx, px, my, py, mz, pz):
    pieces = [
        px[0], mx[0], py[0], my[0], pz[0], mz[0],
        py[2], my[2], py[1], my[1],
        pz[2], mz[2], pz[1], mz[1],
        pz[4], mz[4], pz[3], mz[3],
    ]
    return jnp.concatenate(pieces, axis=1)


AXES = ("gx", "gy", "gz")
TILE = jax.ShapeDtypeStruct((2, 16, 128), jnp.float32)


class Here:
    def __getitem__(self, stage):
        return lax.axis_index(AXES[stage])


HERE = Here()


def store_blocks(ref, parts):
    for i, part in enumerate(parts):
        at, part = part if isinstance(part, tuple) else (i, part)
        if part is None or part.shape != ref.shape[1:]:
            ref[at] = jnp.zeros(ref.shape[1:], ref.dtype)
        if part is not None:
            ref[at, : part.shape[0], : part.shape[1]] = part


def kernel_call(name, body, shapes, *operands, last=False):
    arrays = [pltpu.with_memory_space_constraint(value, pltpu.VMEM) for value in operands if value is not HERE]

    def kernel(*refs):
        given = iter(refs)
        results = body(*[HERE if value is HERE else next(given) for value in operands])
        for ref, result in zip(given, results):
            if isinstance(result, list):
                store_blocks(ref, result)
            elif result.shape != ref.shape:
                lines = result.shape[1] // 128
                for i in range(lines):
                    ref[pl.ds(i, result.shape[0], stride=lines), :] = result[:, 128 * i : 128 * (i + 1)]
            else:
                ref[...] = result

    return pl.pallas_call(
        kernel,
        name=name,
        in_specs=[pl.BlockSpec(memory_space=pltpu.VMEM) for _ in arrays],
        out_specs=[pl.BlockSpec(memory_space=pltpu.VMEM) for _ in shapes],
        out_shape=[shape if last else pltpu.VMEM(shape.shape, shape.dtype) for shape in shapes],
    )(*arrays)


def spread(ahead, behind, place, count):
    return [jnp.where(place < i, ahead, behind) for i in range(count)]


def pair_of(tiles):
    return unpack(tiles[0]), unpack(tiles[1])


MASK = (4, 2, 1)
PAIRS = ((0, 1), (0, 2), (1, 2))


def cubes(kind):
    sizes = [lax.axis_size(axis) for axis in AXES]
    found = {}
    for place in np.ndindex(*sizes):
        corner = tuple((i + kind) // 2 % (size // 2) for i, size in zip(place, sizes))
        member = sum(mask * (i % 2) for mask, i in zip(MASK, place))
        found.setdefault(corner, {})[member] = int(np.ravel_multi_index(place, sizes))
    return [[members[i] for i in range(8)] for members in found.values()]


def heading_of(signs_by_axis):
    return tuple(signs_by_axis.get(axis, 0) for axis in range(3))


class Parity:
    def __init__(self, place):
        parities = [lax.rem(place[axis], 2) for axis in range(3)]
        self.even = [value == 0 for value in parities]
        self.position = sum(mask * value for mask, value in zip(MASK, parities))

    def choose(self, axes, values):
        if len(axes) == 1:
            return jnp.where(self.even[axes[0]], values(0), values(1))
        return jnp.where(
            self.even[axes[0]],
            jnp.where(self.even[axes[1]], values(0, 0), values(0, 1)),
            jnp.where(self.even[axes[1]], values(1, 0), values(1, 1)),
        )

    def own(self, y, axes, kinds):
        def value(*odd):
            return block(y, *heading_of({axis: 1 - 2 * (kind ^ i) for axis, kind, i in zip(axes, kinds, odd)}))

        return self.choose(axes, value)

    def toward(self, axes, signs, by_kinds):
        return self.choose(axes, lambda *odd: by_kinds[tuple(sign ^ i for sign, i in zip(signs, odd))])


def cube_b(y, parity):
    sent = []
    for axis in range(3):
        rest = [other for other in range(3) if other != axis]
        parts = [parity.own(y, (axis,), (1,))]
        for other in rest:
            first, second = sorted((axis, other))
            parts.append(parity.own(y, (first, second), (int(first == axis), int(second == axis))))
        sent.append((MASK[axis], jnp.concatenate(parts, axis=1)))
    for pair in PAIRS:
        sent.append((MASK[pair[0]] | MASK[pair[1]], parity.own(y, pair, (1, 1))))
    return sent


def members(got, parity):
    return {mask: got[parity.position ^ mask][:12] for mask in range(1, 7)}


def edge_at(tile, number):
    return tile[:, FACE + EDGE * number : FACE + EDGE * (number + 1)]


def passed(axis, other):
    return [i for i in range(3) if i != axis].index(other)


def cube_a(y, parity, from_b):
    sent = []
    for axis in range(3):
        parts = [parity.own(y, (axis,), (0,))]
        for other in range(3):
            if other != axis:
                parts.append(edge_at(from_b[MASK[other]], passed(other, axis)))
        sent.append((MASK[axis], jnp.concatenate(parts, axis=1)))
    for pair in PAIRS:
        sent.append((MASK[pair[0]] | MASK[pair[1]], parity.own(y, pair, (0, 0))))
    return sent


def cube_beside(parity, from_a, from_b):
    faces, edges = {}, {}
    for axis in range(3):
        by_kinds = {(0,): from_a[MASK[axis]][:, :FACE], (1,): from_b[MASK[axis]][:, :FACE]}
        for sign in range(2):
            faces[heading_of({axis: 1 - 2 * sign})] = parity.toward((axis,), (sign,), by_kinds)
    for pair in PAIRS:
        mask = MASK[pair[0]] | MASK[pair[1]]
        first, second = pair
        by_kinds = {
            (0, 0): from_a[mask][:, :EDGE],
            (1, 1): from_b[mask][:, :EDGE],
            (0, 1): edge_at(from_a[MASK[first]], passed(first, second)),
            (1, 0): edge_at(from_a[MASK[second]], passed(second, first)),
        }
        for signs in np.ndindex(2, 2):
            heading = heading_of({axis: 1 - 2 * sign for axis, sign in zip(pair, signs)})
            edges[heading] = parity.toward(pair, signs, by_kinds)
    return jnp.concatenate([{**faces, **edges}[heading] for heading in DIRECTIONS], axis=1)


def placed(sent, parity):
    blocks = {mask: value for mask, value in sent}
    return [(parity.position ^ mask, blocks.get(mask)) for mask in range(8)]


def cube_swap(kind, sent, live):
    sent, live = lax.optimization_barrier((sent, live))
    got = lax.all_to_all(sent, AXES, 0, 0, axis_index_groups=cubes(kind), tiled=True)
    return lax.optimization_barrier((got, live))


CUBE = jax.ShapeDtypeStruct((8, 16, 128), jnp.float32)


def exchange_by_cubes(sent, live):
    got, live = cube_swap(1, sent, live)
    live["from_b"] = got

    def second(y, from_b):
        parity = Parity(HERE)
        return (placed(cube_a(y[...], parity, members(from_b, parity)), parity),)

    (sent,) = kernel_call("cube_a", second, (CUBE,), live["y"], live["from_b"])
    got, live = cube_swap(0, sent, live)
    live["from_a"] = got
    return live


def from_cubes(from_a, from_b):
    parity = Parity(HERE)
    return cube_beside(parity, members(from_a, parity), members(from_b, parity))


def gathered(stage, axis, sent, live):
    sent, live = lax.optimization_barrier((sent, live))
    got = lax.all_to_all(sent, axis, 0, 0, tiled=True)
    return lax.optimization_barrier((got, live))


def picked(got, place, stage, number):
    count = got.shape[0]
    here = place[stage]
    before = got[jnp.maximum(here - 1, 0)]
    after = got[jnp.minimum(here + 1, count - 1)]
    low = got[0, 12:16, :]
    for i in range(1, count):
        low = low + got[i, 12:16, :]
    rest = unfold(low)
    return before, after, [rest[:, 2 * EDGE + i : 2 * EDGE + i + 1] for i in range(number)]


def exchange_by_gathers(y, sent, place, number, live):
    sizes = [lax.axis_size(axis) for axis in AXES]

    def blocks(stage):
        return jax.ShapeDtypeStruct((sizes[stage], 16, 128), jnp.float32)

    live = dict(live, y=y)
    got, live = gathered(0, "gx", sent, live)

    def second(y, got, place):
        before, after, sums = picked(got, place, 0, number)
        ahead, behind = messages(1, y[...], unpack(before), unpack(after), None, None, sums)
        return spread(ahead, behind, place[1], sizes[1]), [before, after]

    sent, x_tiles = kernel_call("second_sum", second, (blocks(1), TILE), live["y"], got, HERE)
    live["x_tiles"] = x_tiles
    got, live = gathered(1, "gy", sent, live)

    def third(y, x_tiles, got, place):
        before, after, sums = picked(got, place, 1, number)
        ahead, behind = messages(2, y[...], *pair_of(x_tiles), unpack(before), unpack(after), sums)
        return spread(ahead, behind, place[2], sizes[2]), [before, after]

    sent, y_tiles = kernel_call("third_sum", third, (blocks(2), TILE), live["y"], live["x_tiles"], got, HERE)
    live["y_tiles"] = y_tiles
    return gathered(2, "gz", sent, live)


def from_gathers(got, x_tiles, y_tiles, place, number):
    before, after, sums = picked(got, place, 2, number)
    return beside(*pair_of(x_tiles), *pair_of(y_tiles), unpack(before), unpack(after)), sums


def load_call(loads, counts, signs, shapes):
    def kernel(loads_in, counts_in, signs_in, y, sent, alive, signed, lines, counts, signs, arrived):
        copies = [
            pltpu.make_async_copy(source, target, arrived.at[i])
            for i, (source, target) in enumerate(((loads_in, lines), (counts_in, counts), (signs_in, signs)))
        ]
        for copy in copies:
            copy.start()
        copies[0].wait()
        cases = y.shape[0]
        folds = y.shape[1] // 128
        values = jnp.concatenate([lines[pl.ds(i, cases, stride=folds), :] for i in range(folds)], axis=1)
        y[...] = values
        parity = Parity(HERE)
        store_blocks(sent, placed(cube_b(values, parity), parity))
        copies[1].wait()
        position = lax.broadcasted_iota(jnp.int32, (1, FACE), 1)
        alive[...] = jnp.concatenate(
            [
                (position[:, : CAPACITY[course]] < counts[:, course : course + 1]).astype(jnp.float32)
                for course in range(len(DIRECTIONS))
            ],
            axis=1,
        )
        copies[2].wait()
        signed[...] = signs[...].astype(jnp.float32) * alive[...]

    return pl.pallas_call(
        kernel,
        name="load_blocks",
        in_specs=[pl.BlockSpec(memory_space=pl.ANY) for _ in range(3)],
        out_specs=[pl.BlockSpec(memory_space=pltpu.VMEM) for _ in shapes],
        out_shape=[pltpu.VMEM(shape.shape, shape.dtype) for shape in shapes],
        scratch_shapes=[
            pltpu.VMEM(loads.shape, loads.dtype),
            pltpu.VMEM(counts.shape, counts.dtype),
            pltpu.VMEM(signs.shape, signs.dtype),
            pltpu.SemaphoreType.DMA((3,)),
        ],
    )(loads, counts, signs)


def per_device(loads, dual_ops, precond, counts, signs):
    place = HERE
    dual, pre = dual_ops[0, 0, 0], precond[0, 0, 0]
    loads = loads[0, 0, 0]
    sizes = [lax.axis_size(axis) for axis in AXES]
    vector = jax.ShapeDtypeStruct(loads.shape, jnp.float32)
    rounded = jax.ShapeDtypeStruct(loads.shape, jnp.bfloat16)
    column = jax.ShapeDtypeStruct((loads.shape[0], 1), jnp.float32)
    first_blocks = jax.ShapeDtypeStruct((sizes[0], 16, 128), jnp.float32)

    def times(scaled, matrix):
        return jnp.dot(scaled, matrix, preferred_element_type=jnp.float32)

    def dot(left, right):
        return jnp.sum(left * right, axis=1, keepdims=True)

    row = jax.ShapeDtypeStruct((1, loads.shape[1]), jnp.float32)
    live = dict(dual=dual, pre=pre)
    live["y"], sent, live["alive"], live["signed"] = load_call(
        loads.reshape(-1, 128), counts[0, 0], signs[0, 0], (vector, CUBE, row, row)
    )
    live = exchange_by_cubes(sent, live)

    def assemble(y, alive, signed, from_a, from_b):
        whole = alive[...] * (y[...] + from_cubes(from_a, from_b))
        return whole, (signed[...] * whole).astype(jnp.bfloat16)

    names = ("y", "alive", "signed", "from_a", "from_b")
    live["residual"], scaled = kernel_call("begin", assemble, (vector, rounded), *[live.pop(name) if name[0] in "fy" else live[name] for name in names])

    def precond_blocks(product, signed, residual):
        y = signed[...] * product[...]
        parity = Parity(HERE)
        return y, dot(residual[...], y), placed(cube_b(y, parity), parity)

    live["y"], live["gamma_part"], sent = kernel_call(
        "precond_blocks",
        precond_blocks,
        (vector, column, CUBE),
        times(scaled, live["pre"]),
        live["signed"],
        live["residual"],
    )
    live = exchange_by_cubes(sent, live)
    live["direction"], scaled = kernel_call("aim", assemble, (vector, rounded), *[live.pop(name) if name[0] in "fy" else live[name] for name in names])

    def image_blocks(product, signed, direction, gamma_part, place):
        y = signed[...] * product[...]
        sums = (gamma_part[...], dot(direction[...], y))
        return y, spread(*messages(0, y, None, None, None, None, sums), place[0], sizes[0])

    y, sent = kernel_call(
        "image_blocks",
        image_blocks,
        (vector, first_blocks),
        times(scaled, live["dual"]),
        live["signed"],
        live["direction"],
        live.pop("gamma_part"),
        place,
    )
    got, live = exchange_by_gathers(y, sent, place, 2, live)

    def first_step(got, x_tiles, y_tiles, y, place, alive, signed, direction, residual):
        near, (gamma, curvature) = from_gathers(got, x_tiles, y_tiles, place, 2)
        image = alive[...] * (y[...] + near)
        step = gamma / curvature
        left = residual[...] - step * image
        return step * direction[...], left, (signed[...] * left).astype(jnp.bfloat16), gamma

    names = ("x_tiles", "y_tiles", "y", "place", "alive", "signed", "direction", "residual")
    live["multipliers"], live["residual"], scaled, live["gamma"] = kernel_call(
        "first_step", first_step, (vector, vector, rounded, column), got, *[live[name] if name != "place" else HERE for name in names]
    )

    def sum_blocks(product, signed, left, place):
        y = signed[...] * product[...]
        sums = (dot(left[...], y),)
        return y, spread(*messages(0, y, None, None, None, None, sums), place[0], sizes[0])

    for iteration in range(1, ITERS):
        y, sent = kernel_call(
            "smooth_blocks",
            sum_blocks,
            (vector, first_blocks),
            times(scaled, live["pre"]),
            live["signed"],
            live["residual"],
            HERE,
        )
        got, live = exchange_by_gathers(y, sent, HERE, 1, live)

        def turn(got, x_tiles, y_tiles, y, place, alive, signed, direction, gamma_old):
            near, (gamma,) = from_gathers(got, x_tiles, y_tiles, place, 1)
            smoothed = alive[...] * (y[...] + near)
            turned = smoothed + (gamma / gamma_old[...]) * direction[...]
            return turned, (signed[...] * turned).astype(jnp.bfloat16), gamma

        names = ("x_tiles", "y_tiles", "y", "place", "alive", "signed", "direction", "gamma")
        live["direction"], scaled, live["gamma"] = kernel_call(
            "turn", turn, (vector, rounded, column), got, *[live[name] if name != "place" else HERE for name in names]
        )
        y, sent = kernel_call(
            "sum_blocks",
            sum_blocks,
            (vector, first_blocks),
            times(scaled, live["dual"]),
            live["signed"],
            live["direction"],
            HERE,
        )
        got, live = exchange_by_gathers(y, sent, HERE, 1, live)

        def advance(got, x_tiles, y_tiles, y, place, alive, signed, direction, gamma, multipliers, residual):
            near, (curvature,) = from_gathers(got, x_tiles, y_tiles, place, 1)
            image = alive[...] * (y[...] + near)
            step = gamma[...] / curvature
            left = residual[...] - step * image
            results = (multipliers[...] + step * direction[...], left)
            if iteration < ITERS - 1:
                results += ((signed[...] * left).astype(jnp.bfloat16),)
            return results

        lines = jax.ShapeDtypeStruct((loads.size // 128, 128), jnp.float32)
        shapes = (vector, vector, rounded) if iteration < ITERS - 1 else (lines, lines)
        names = ("x_tiles", "y_tiles", "y", "place", "alive", "signed", "direction", "gamma", "multipliers", "residual")
        live["multipliers"], live["residual"], *rest = kernel_call(
            "advance",
            advance,
            shapes,
            got,
            *[live[name] if name != "place" else HERE for name in names],
            last=iteration == ITERS - 1,
        )
        if rest:
            scaled = rest[0]
    whole = (1, 1, 1, *loads.shape)
    return (live["multipliers"].reshape(whole), live["residual"].reshape(whole))


def solution(mesh):
    placed = (
        P("gx", "gy", "gz", None, None),
        P("gx", "gy", "gz", None, None),
        P("gx", "gy", "gz", None, None),
        P("gx", "gy", "gz", None),
        P("gx", "gy", "gz", None),
    )
    return jax.shard_map(
        per_device,
        mesh=mesh,
        in_specs=placed,
        out_specs=(P("gx", "gy", "gz", None, None), P("gx", "gy", "gz", None, None)),
        check_vma=False,
    )
```

```python
import jax
import jax.numpy as jnp
import numpy as np
from jax import lax
from jax.experimental import pallas as pl
from jax.experimental.pallas import tpu as pltpu
from jax.sharding import PartitionSpec as P

FACE = 96
EDGE = 16
ITERS = 2


DIRECTIONS = (
    (1, 0, 0),
    (-1, 0, 0),
    (0, 1, 0),
    (0, -1, 0),
    (0, 0, 1),
    (0, 0, -1),
    (1, 1, 0),
    (1, -1, 0),
    (-1, 1, 0),
    (-1, -1, 0),
    (1, 0, 1),
    (1, 0, -1),
    (-1, 0, 1),
    (-1, 0, -1),
    (0, 1, 1),
    (0, 1, -1),
    (0, -1, 1),
    (0, -1, -1),
)


def block_table():
    capacity = [FACE] * 6 + [EDGE] * 12
    offsets = [sum(capacity[:course]) for course in range(18)]
    return (capacity, offsets)


CAPACITY, OFFSETS = block_table()


def block(values, *heading):
    course = DIRECTIONS.index(heading)
    return values[:, OFFSETS[course] : OFFSETS[course] + CAPACITY[course]]


THIRD = 42


def pack(face, edge_a, edge_b, edge_c, edge_d, sums):
    top = jnp.concatenate([face, edge_a, edge_b], axis=1)
    rest = jnp.concatenate([edge_c, edge_d, *sums], axis=1)
    rest = jnp.pad(rest, ((0, 0), (0, THIRD - rest.shape[1])))
    low = jnp.concatenate([rest[0:4], rest[4:8], rest[8:12]], axis=1)
    low = jnp.pad(low, ((0, 0), (0, 128 - 3 * THIRD)))
    return jnp.concatenate([top, low], axis=0)


def unfold(low):
    return jnp.concatenate([low[:, THIRD * i : THIRD * (i + 1)] for i in range(3)], axis=0)


def unpack(tile):
    rest = unfold(tile[12:16])
    return (
        tile[:12, :FACE],
        tile[:12, FACE : FACE + EDGE],
        tile[:12, FACE + EDGE : FACE + 2 * EDGE],
        rest[:, :EDGE],
        rest[:, EDGE : 2 * EDGE],
    )


def messages(stage, y, mx, px, my, py, sums):
    if stage == 0:
        ahead = (block(y, 1, 0, 0), block(y, 1, 1, 0), block(y, 1, -1, 0), block(y, 1, 0, 1), block(y, 1, 0, -1))
        behind = (block(y, -1, 0, 0), block(y, -1, 1, 0), block(y, -1, -1, 0), block(y, -1, 0, 1), block(y, -1, 0, -1))
    elif stage == 1:
        ahead = (block(y, 0, 1, 0), mx[1], px[1], block(y, 0, 1, 1), block(y, 0, 1, -1))
        behind = (block(y, 0, -1, 0), mx[2], px[2], block(y, 0, -1, 1), block(y, 0, -1, -1))
    else:
        ahead = (block(y, 0, 0, 1), mx[3], px[3], my[3], py[3])
        behind = (block(y, 0, 0, -1), mx[4], px[4], my[4], py[4])
    return pack(*ahead, sums), pack(*behind, sums)


def beside(mx, px, my, py, mz, pz):
    pieces = [
        px[0], mx[0], py[0], my[0], pz[0], mz[0],
        py[2], my[2], py[1], my[1],
        pz[4], mz[4], pz[3], mz[3],
        pz[2], mz[2], pz[1], mz[1],
    ]
    return jnp.concatenate(pieces, axis=1)


def turned(values):
    swapped = jnp.concatenate([block(values, y, x, z) for x, y, z in DIRECTIONS], axis=1)
    return jnp.where(lax.rem(HERE[2], 2) == 0, values, swapped)


def line_place(stage):
    if stage == 2:
        return HERE[2]
    return jnp.where(lax.rem(HERE[2], 2) == 0, HERE[stage], HERE[1 - stage])


def lines_of(stage):
    sizes = [lax.axis_size(axis) for axis in AXES]
    assert sizes[0] == sizes[1]
    groups = []
    for z in range(sizes[2]):
        for fixed in range(sizes[0]):
            places = [(i, fixed, z) if (stage + z) % 2 == 0 else (fixed, i, z) for i in range(sizes[0])]
            groups.append([int(np.ravel_multi_index(place, sizes)) for place in places])
    return groups


AXES = ("gx", "gy", "gz")
TILE = jax.ShapeDtypeStruct((2, 16, 128), jnp.float32)


class Here:
    def __getitem__(self, stage):
        return lax.axis_index(AXES[stage])


HERE = Here()


def store_blocks(ref, parts):
    for i, part in enumerate(parts):
        at, part = part if isinstance(part, tuple) else (i, part)
        if part is None or part.shape != ref.shape[1:]:
            ref[at] = jnp.zeros(ref.shape[1:], ref.dtype)
        if part is not None:
            ref[at, : part.shape[0], : part.shape[1]] = part


def kernel_call(name, body, shapes, *operands, last=False):
    arrays = [pltpu.with_memory_space_constraint(value, pltpu.VMEM) for value in operands if value is not HERE]

    def kernel(*refs):
        given = iter(refs)
        results = body(*[HERE if value is HERE else next(given) for value in operands])
        for ref, result in zip(given, results):
            if isinstance(result, list):
                store_blocks(ref, result)
            elif result.shape != ref.shape:
                lines = result.shape[1] // 128
                for i in range(lines):
                    ref[pl.ds(i, result.shape[0], stride=lines), :] = result[:, 128 * i : 128 * (i + 1)]
            else:
                ref[...] = result

    return pl.pallas_call(
        kernel,
        name=name,
        in_specs=[pl.BlockSpec(memory_space=pltpu.VMEM) for _ in arrays],
        out_specs=[pl.BlockSpec(memory_space=pltpu.VMEM) for _ in shapes],
        out_shape=[shape if last else pltpu.VMEM(shape.shape, shape.dtype) for shape in shapes],
    )(*arrays)


def spread(ahead, behind, place, count):
    return [jnp.where(place < i, ahead, behind) for i in range(count)]


def pair_of(tiles):
    return unpack(tiles[0]), unpack(tiles[1])


MASK = (4, 2, 1)
PAIRS = ((0, 1), (0, 2), (1, 2))


def cubes(kind):
    sizes = [lax.axis_size(axis) for axis in AXES]
    found = {}
    for place in np.ndindex(*sizes):
        corner = tuple((i + kind) // 2 % (size // 2) for i, size in zip(place, sizes))
        member = sum(mask * (i % 2) for mask, i in zip(MASK, place))
        found.setdefault(corner, {})[member] = int(np.ravel_multi_index(place, sizes))
    return [[members[i] for i in range(8)] for members in found.values()]


def heading_of(signs_by_axis):
    return tuple(signs_by_axis.get(axis, 0) for axis in range(3))


class Parity:
    def __init__(self, place):
        parities = [lax.rem(place[axis], 2) for axis in range(3)]
        self.even = [value == 0 for value in parities]
        self.position = sum(mask * value for mask, value in zip(MASK, parities))

    def choose(self, axes, values):
        if len(axes) == 1:
            return jnp.where(self.even[axes[0]], values(0), values(1))
        return jnp.where(
            self.even[axes[0]],
            jnp.where(self.even[axes[1]], values(0, 0), values(0, 1)),
            jnp.where(self.even[axes[1]], values(1, 0), values(1, 1)),
        )

    def own(self, y, axes, kinds):
        def value(*odd):
            return block(y, *heading_of({axis: 1 - 2 * (kind ^ i) for axis, kind, i in zip(axes, kinds, odd)}))

        return self.choose(axes, value)

    def toward(self, axes, signs, by_kinds):
        return self.choose(axes, lambda *odd: by_kinds[tuple(sign ^ i for sign, i in zip(signs, odd))])


def cube_b(y, parity):
    sent = []
    for axis in range(3):
        rest = [other for other in range(3) if other != axis]
        parts = [parity.own(y, (axis,), (1,))]
        for other in rest:
            first, second = sorted((axis, other))
            parts.append(parity.own(y, (first, second), (int(first == axis), int(second == axis))))
        sent.append((MASK[axis], jnp.concatenate(parts, axis=1)))
    for pair in PAIRS:
        sent.append((MASK[pair[0]] | MASK[pair[1]], parity.own(y, pair, (1, 1))))
    return sent


def members(got, parity):
    return {mask: got[parity.position ^ mask][:12] for mask in range(1, 7)}


def edge_at(tile, number):
    return tile[:, FACE + EDGE * number : FACE + EDGE * (number + 1)]


def passed(axis, other):
    return [i for i in range(3) if i != axis].index(other)


def cube_a(y, parity, from_b):
    sent = []
    for axis in range(3):
        parts = [parity.own(y, (axis,), (0,))]
        for other in range(3):
            if other != axis:
                parts.append(edge_at(from_b[MASK[other]], passed(other, axis)))
        sent.append((MASK[axis], jnp.concatenate(parts, axis=1)))
    for pair in PAIRS:
        sent.append((MASK[pair[0]] | MASK[pair[1]], parity.own(y, pair, (0, 0))))
    return sent


def cube_beside(parity, from_a, from_b):
    faces, edges = {}, {}
    for axis in range(3):
        by_kinds = {(0,): from_a[MASK[axis]][:, :FACE], (1,): from_b[MASK[axis]][:, :FACE]}
        for sign in range(2):
            faces[heading_of({axis: 1 - 2 * sign})] = parity.toward((axis,), (sign,), by_kinds)
    for pair in PAIRS:
        mask = MASK[pair[0]] | MASK[pair[1]]
        first, second = pair
        by_kinds = {
            (0, 0): from_a[mask][:, :EDGE],
            (1, 1): from_b[mask][:, :EDGE],
            (0, 1): edge_at(from_a[MASK[first]], passed(first, second)),
            (1, 0): edge_at(from_a[MASK[second]], passed(second, first)),
        }
        for signs in np.ndindex(2, 2):
            heading = heading_of({axis: 1 - 2 * sign for axis, sign in zip(pair, signs)})
            edges[heading] = parity.toward(pair, signs, by_kinds)
    return jnp.concatenate([{**faces, **edges}[heading] for heading in DIRECTIONS], axis=1)


def placed(sent, parity):
    blocks = {mask: value for mask, value in sent}
    return [(parity.position ^ mask, blocks.get(mask)) for mask in range(8)]


def cube_swap(kind, sent, live):
    sent, live = lax.optimization_barrier((sent, live))
    got = lax.all_to_all(sent, AXES, 0, 0, axis_index_groups=cubes(kind), tiled=True)
    return lax.optimization_barrier((got, live))


CUBE = jax.ShapeDtypeStruct((8, 16, 128), jnp.float32)


def exchange_by_cubes(sent, live):
    got, live = cube_swap(1, sent, live)
    live["from_b"] = got

    def second(y, from_b):
        parity = Parity(HERE)
        return (placed(cube_a(y[...], parity, members(from_b, parity)), parity),)

    (sent,) = kernel_call("cube_a", second, (CUBE,), live["y"], live["from_b"])
    got, live = cube_swap(0, sent, live)
    live["from_a"] = got
    return live


def from_cubes(from_a, from_b):
    parity = Parity(HERE)
    return cube_beside(parity, members(from_a, parity), members(from_b, parity))


def gathered(stage, axis, sent, live):
    sent, live = lax.optimization_barrier((sent, live))
    if stage < 2:
        got = lax.all_to_all(sent, AXES, 0, 0, axis_index_groups=lines_of(stage), tiled=True)
    else:
        got = lax.all_to_all(sent, axis, 0, 0, tiled=True)
    return lax.optimization_barrier((got, live))


def picked(got, place, stage, number):
    count = got.shape[0]
    here = line_place(stage)
    before = got[jnp.maximum(here - 1, 0)]
    after = got[jnp.minimum(here + 1, count - 1)]
    low = got[0, 12:16, :]
    for i in range(1, count):
        low = low + got[i, 12:16, :]
    rest = unfold(low)
    return before, after, [rest[:, 2 * EDGE + i : 2 * EDGE + i + 1] for i in range(number)]


def exchange_by_gathers(y, sent, place, number, live):
    sizes = [lax.axis_size(axis) for axis in AXES]

    def blocks(stage):
        return jax.ShapeDtypeStruct((sizes[stage], 16, 128), jnp.float32)

    live = dict(live, y=y)
    got, live = gathered(0, "gx", sent, live)

    def second(y, got, place):
        before, after, sums = picked(got, place, 0, number)
        ahead, behind = messages(1, y[...], unpack(before), unpack(after), None, None, sums)
        return spread(ahead, behind, line_place(1), sizes[1]), [before, after]

    sent, x_tiles = kernel_call("second_sum", second, (blocks(1), TILE), live["y"], got, HERE)
    live["x_tiles"] = x_tiles
    got, live = gathered(1, "gy", sent, live)

    def third(y, x_tiles, got, place):
        before, after, sums = picked(got, place, 1, number)
        ahead, behind = messages(2, y[...], *pair_of(x_tiles), unpack(before), unpack(after), sums)
        return spread(ahead, behind, line_place(2), sizes[2]), [before, after]

    sent, y_tiles = kernel_call("third_sum", third, (blocks(2), TILE), live["y"], live["x_tiles"], got, HERE)
    live["y_tiles"] = y_tiles
    return gathered(2, "gz", sent, live)


def from_gathers(got, x_tiles, y_tiles, place, number):
    before, after, sums = picked(got, place, 2, number)
    return beside(*pair_of(x_tiles), *pair_of(y_tiles), unpack(before), unpack(after)), sums


def load_call(loads, counts, signs, shapes):
    def kernel(loads_in, counts_in, signs_in, y, sent, alive, signed, lines, counts, signs, arrived):
        copies = [
            pltpu.make_async_copy(source, target, arrived.at[i])
            for i, (source, target) in enumerate(((loads_in, lines), (counts_in, counts), (signs_in, signs)))
        ]
        for copy in copies:
            copy.start()
        copies[0].wait()
        cases = y.shape[0]
        folds = y.shape[1] // 128
        values = jnp.concatenate([lines[pl.ds(i, cases, stride=folds), :] for i in range(folds)], axis=1)
        y[...] = values
        parity = Parity(HERE)
        store_blocks(sent, placed(cube_b(values, parity), parity))
        copies[1].wait()
        position = lax.broadcasted_iota(jnp.int32, (1, FACE), 1)
        alive[...] = jnp.concatenate(
            [
                (position[:, : CAPACITY[course]] < counts[:, course : course + 1]).astype(jnp.float32)
                for course in range(len(DIRECTIONS))
            ],
            axis=1,
        )
        copies[2].wait()
        signed[...] = signs[...].astype(jnp.float32) * alive[...]

    return pl.pallas_call(
        kernel,
        name="load_blocks",
        in_specs=[pl.BlockSpec(memory_space=pl.ANY) for _ in range(3)],
        out_specs=[pl.BlockSpec(memory_space=pltpu.VMEM) for _ in shapes],
        out_shape=[pltpu.VMEM(shape.shape, shape.dtype) for shape in shapes],
        scratch_shapes=[
            pltpu.VMEM(loads.shape, loads.dtype),
            pltpu.VMEM(counts.shape, counts.dtype),
            pltpu.VMEM(signs.shape, signs.dtype),
            pltpu.SemaphoreType.DMA((3,)),
        ],
    )(loads, counts, signs)


def per_device(loads, dual_ops, precond, counts, signs):
    place = HERE
    dual, pre = dual_ops[0, 0, 0], precond[0, 0, 0]
    loads = loads[0, 0, 0]
    sizes = [lax.axis_size(axis) for axis in AXES]
    vector = jax.ShapeDtypeStruct(loads.shape, jnp.float32)
    rounded = jax.ShapeDtypeStruct(loads.shape, jnp.bfloat16)
    column = jax.ShapeDtypeStruct((loads.shape[0], 1), jnp.float32)
    first_blocks = jax.ShapeDtypeStruct((sizes[0], 16, 128), jnp.float32)

    def times(scaled, matrix):
        return jnp.dot(scaled, matrix, preferred_element_type=jnp.float32)

    def dot(left, right):
        return jnp.sum(left * right, axis=1, keepdims=True)

    row = jax.ShapeDtypeStruct((1, loads.shape[1]), jnp.float32)
    live = dict(dual=dual, pre=pre)
    live["y"], sent, live["alive"], live["signed"] = load_call(
        loads.reshape(-1, 128), counts[0, 0], signs[0, 0], (vector, CUBE, row, row)
    )
    live = exchange_by_cubes(sent, live)

    def assemble(y, alive, signed, from_a, from_b):
        whole = alive[...] * (y[...] + from_cubes(from_a, from_b))
        return whole, (signed[...] * whole).astype(jnp.bfloat16)

    names = ("y", "alive", "signed", "from_a", "from_b")
    live["residual"], scaled = kernel_call("begin", assemble, (vector, rounded), *[live.pop(name) if name[0] in "fy" else live[name] for name in names])

    def precond_blocks(product, signed, residual):
        y = signed[...] * product[...]
        parity = Parity(HERE)
        return y, dot(residual[...], y), placed(cube_b(y, parity), parity)

    live["y"], live["gamma_part"], sent = kernel_call(
        "precond_blocks",
        precond_blocks,
        (vector, column, CUBE),
        times(scaled, live["pre"]),
        live["signed"],
        live["residual"],
    )
    live = exchange_by_cubes(sent, live)
    live["direction"], scaled = kernel_call("aim", assemble, (vector, rounded), *[live.pop(name) if name[0] in "fy" else live[name] for name in names])

    def image_blocks(product, signed, direction, gamma_part, place):
        y = signed[...] * product[...]
        sums = (gamma_part[...], dot(direction[...], y))
        y = turned(y)
        return y, spread(*messages(0, y, None, None, None, None, sums), line_place(0), sizes[0])

    y, sent = kernel_call(
        "image_blocks",
        image_blocks,
        (vector, first_blocks),
        times(scaled, live["dual"]),
        live["signed"],
        live["direction"],
        live.pop("gamma_part"),
        place,
    )
    got, live = exchange_by_gathers(y, sent, place, 2, live)

    def first_step(got, x_tiles, y_tiles, y, place, alive, signed, direction, residual):
        near, (gamma, curvature) = from_gathers(got, x_tiles, y_tiles, place, 2)
        image = alive[...] * turned(y[...] + near)
        step = gamma / curvature
        left = residual[...] - step * image
        return step * direction[...], left, (signed[...] * left).astype(jnp.bfloat16), gamma

    names = ("x_tiles", "y_tiles", "y", "place", "alive", "signed", "direction", "residual")
    live["multipliers"], live["residual"], scaled, live["gamma"] = kernel_call(
        "first_step", first_step, (vector, vector, rounded, column), got, *[live[name] if name != "place" else HERE for name in names]
    )

    def sum_blocks(product, signed, left, place):
        y = signed[...] * product[...]
        sums = (dot(left[...], y),)
        y = turned(y)
        return y, spread(*messages(0, y, None, None, None, None, sums), line_place(0), sizes[0])

    for iteration in range(1, ITERS):
        y, sent = kernel_call(
            "smooth_blocks",
            sum_blocks,
            (vector, first_blocks),
            times(scaled, live["pre"]),
            live["signed"],
            live["residual"],
            HERE,
        )
        got, live = exchange_by_gathers(y, sent, HERE, 1, live)

        def turn(got, x_tiles, y_tiles, y, place, alive, signed, direction, gamma_old):
            near, (gamma,) = from_gathers(got, x_tiles, y_tiles, place, 1)
            smoothed = alive[...] * turned(y[...] + near)
            fresh = smoothed + (gamma / gamma_old[...]) * direction[...]
            return fresh, (signed[...] * fresh).astype(jnp.bfloat16), gamma

        names = ("x_tiles", "y_tiles", "y", "place", "alive", "signed", "direction", "gamma")
        live["direction"], scaled, live["gamma"] = kernel_call(
            "turn", turn, (vector, rounded, column), got, *[live[name] if name != "place" else HERE for name in names]
        )
        y, sent = kernel_call(
            "sum_blocks",
            sum_blocks,
            (vector, first_blocks),
            times(scaled, live["dual"]),
            live["signed"],
            live["direction"],
            HERE,
        )
        got, live = exchange_by_gathers(y, sent, HERE, 1, live)

        def advance(got, x_tiles, y_tiles, y, place, alive, signed, direction, gamma, multipliers, residual):
            near, (curvature,) = from_gathers(got, x_tiles, y_tiles, place, 1)
            image = alive[...] * turned(y[...] + near)
            step = gamma[...] / curvature
            left = residual[...] - step * image
            results = (multipliers[...] + step * direction[...], left)
            if iteration < ITERS - 1:
                results += ((signed[...] * left).astype(jnp.bfloat16),)
            return results

        lines = jax.ShapeDtypeStruct((loads.size // 128, 128), jnp.float32)
        shapes = (vector, vector, rounded) if iteration < ITERS - 1 else (lines, lines)
        names = ("x_tiles", "y_tiles", "y", "place", "alive", "signed", "direction", "gamma", "multipliers", "residual")
        live["multipliers"], live["residual"], *rest = kernel_call(
            "advance",
            advance,
            shapes,
            got,
            *[live[name] if name != "place" else HERE for name in names],
            last=iteration == ITERS - 1,
        )
        if rest:
            scaled = rest[0]
    whole = (1, 1, 1, *loads.shape)
    return (live["multipliers"].reshape(whole), live["residual"].reshape(whole))


def solution(mesh):
    placed = (
        P("gx", "gy", "gz", None, None),
        P("gx", "gy", "gz", None, None),
        P("gx", "gy", "gz", None, None),
        P("gx", "gy", "gz", None),
        P("gx", "gy", "gz", None),
    )
    return jax.shard_map(
        per_device,
        mesh=mesh,
        in_specs=placed,
        out_specs=(P("gx", "gy", "gz", None, None), P("gx", "gy", "gz", None, None)),
        check_vma=False,
    )
```

```python
import jax
import jax.numpy as jnp
import numpy as np
from jax import lax
from jax.experimental import pallas as pl
from jax.experimental.pallas import tpu as pltpu
from jax.sharding import PartitionSpec as P

FACE = 96
EDGE = 16
ITERS = 2


DIRECTIONS = (
    (1, 0, 0),
    (-1, 0, 0),
    (0, 1, 0),
    (0, -1, 0),
    (0, 0, 1),
    (0, 0, -1),
    (1, 1, 0),
    (1, -1, 0),
    (-1, 1, 0),
    (-1, -1, 0),
    (1, 0, 1),
    (1, 0, -1),
    (-1, 0, 1),
    (-1, 0, -1),
    (0, 1, 1),
    (0, 1, -1),
    (0, -1, 1),
    (0, -1, -1),
)


def block_table():
    capacity = [FACE] * 6 + [EDGE] * 12
    offsets = [sum(capacity[:course]) for course in range(18)]
    return (capacity, offsets)


CAPACITY, OFFSETS = block_table()


def block(values, *heading):
    course = DIRECTIONS.index(heading)
    return values[:, OFFSETS[course] : OFFSETS[course] + CAPACITY[course]]


THIRD = 42


def pack(face, edge_a, edge_b, edge_c, edge_d, sums):
    top = jnp.concatenate([face, edge_a, edge_b], axis=1)
    rest = jnp.concatenate([edge_c, edge_d, *sums], axis=1)
    rest = jnp.pad(rest, ((0, 0), (0, THIRD - rest.shape[1])))
    low = jnp.concatenate([rest[0:4], rest[4:8], rest[8:12]], axis=1)
    low = jnp.pad(low, ((0, 0), (0, 128 - 3 * THIRD)))
    return jnp.concatenate([top, low], axis=0)


def unfold(low):
    return jnp.concatenate([low[:, THIRD * i : THIRD * (i + 1)] for i in range(3)], axis=0)


def unpack(tile):
    rest = unfold(tile[12:16])
    return (
        tile[:12, :FACE],
        tile[:12, FACE : FACE + EDGE],
        tile[:12, FACE + EDGE : FACE + 2 * EDGE],
        rest[:, :EDGE],
        rest[:, EDGE : 2 * EDGE],
    )


def messages(stage, y, mx, px, my, py, sums):
    if stage == 0:
        ahead = (block(y, 1, 0, 0), block(y, 1, 1, 0), block(y, 1, -1, 0), block(y, 1, 0, 1), block(y, 1, 0, -1))
        behind = (block(y, -1, 0, 0), block(y, -1, 1, 0), block(y, -1, -1, 0), block(y, -1, 0, 1), block(y, -1, 0, -1))
    elif stage == 1:
        ahead = (block(y, 0, 1, 0), mx[1], px[1], block(y, 0, 1, 1), block(y, 0, 1, -1))
        behind = (block(y, 0, -1, 0), mx[2], px[2], block(y, 0, -1, 1), block(y, 0, -1, -1))
    else:
        ahead = (block(y, 0, 0, 1), mx[3], px[3], my[3], py[3])
        behind = (block(y, 0, 0, -1), mx[4], px[4], my[4], py[4])
    return pack(*ahead, sums), pack(*behind, sums)


def beside(mx, px, my, py, mz, pz):
    pieces = [
        px[0], mx[0], py[0], my[0], pz[0], mz[0],
        py[2], my[2], py[1], my[1],
        pz[4], mz[4], pz[3], mz[3],
        pz[2], mz[2], pz[1], mz[1],
    ]
    return jnp.concatenate(pieces, axis=1)


def turned(values):
    swapped = jnp.concatenate([block(values, y, x, z) for x, y, z in DIRECTIONS], axis=1)
    return jnp.where(lax.rem(HERE[2], 2) == 0, values, swapped)


def line_place(stage):
    if stage == 2:
        return HERE[2]
    return jnp.where(lax.rem(HERE[2], 2) == 0, HERE[stage], HERE[1 - stage])


def lines_of(stage):
    sizes = [lax.axis_size(axis) for axis in AXES]
    assert sizes[0] == sizes[1]
    groups = []
    for z in range(sizes[2]):
        for fixed in range(sizes[0]):
            places = [(i, fixed, z) if (stage + z) % 2 == 0 else (fixed, i, z) for i in range(sizes[0])]
            groups.append([int(np.ravel_multi_index(place, sizes)) for place in places])
    return groups


AXES = ("gx", "gy", "gz")
TILE = jax.ShapeDtypeStruct((2, 16, 128), jnp.float32)


class Here:
    def __getitem__(self, stage):
        return lax.axis_index(AXES[stage])


HERE = Here()


def store_blocks(ref, parts):
    for i, part in enumerate(parts):
        at, part = part if isinstance(part, tuple) else (i, part)
        if part is None or part.shape != ref.shape[1:]:
            ref[at] = jnp.zeros(ref.shape[1:], ref.dtype)
        if part is not None:
            ref[at, : part.shape[0], : part.shape[1]] = part


def kernel_call(name, body, shapes, *operands, last=False):
    arrays = [pltpu.with_memory_space_constraint(value, pltpu.VMEM) for value in operands if value is not HERE]

    def kernel(*refs):
        given = iter(refs)
        results = body(*[HERE if value is HERE else next(given) for value in operands])
        for ref, result in zip(given, results):
            if isinstance(result, list):
                store_blocks(ref, result)
            elif result.shape != ref.shape:
                lines = result.shape[1] // 128
                for i in range(lines):
                    ref[pl.ds(i, result.shape[0], stride=lines), :] = result[:, 128 * i : 128 * (i + 1)]
            else:
                ref[...] = result

    if last:

        def leaving(*refs):
            count = len(arrays)
            given, left, kept, sent = refs[:count], refs[count:-len(shapes) - 1], refs[-len(shapes) - 1 : -1], refs[-1]
            kernel(*given, *kept)
            copies = [pltpu.make_async_copy(*pair, sent.at[i]) for i, pair in enumerate(zip(kept, left))]
            for copy in copies:
                copy.start()
            for copy in copies:
                copy.wait()

        return pl.pallas_call(
            leaving,
            name=name,
            in_specs=[pl.BlockSpec(memory_space=pltpu.VMEM) for _ in arrays],
            out_specs=[pl.BlockSpec(memory_space=pl.ANY) for _ in shapes],
            out_shape=list(shapes),
            scratch_shapes=[
                *[pltpu.VMEM(shape.shape, shape.dtype) for shape in shapes],
                pltpu.SemaphoreType.DMA((len(shapes),)),
            ],
        )(*arrays)
    return pl.pallas_call(
        kernel,
        name=name,
        in_specs=[pl.BlockSpec(memory_space=pltpu.VMEM) for _ in arrays],
        out_specs=[pl.BlockSpec(memory_space=pltpu.VMEM) for _ in shapes],
        out_shape=[pltpu.VMEM(shape.shape, shape.dtype) for shape in shapes],
    )(*arrays)


def spread(ahead, behind, place, count):
    return [jnp.where(place < i, ahead, behind) for i in range(count)]


def pair_of(tiles):
    return unpack(tiles[0]), unpack(tiles[1])


MASK = (4, 2, 1)
PAIRS = ((0, 1), (0, 2), (1, 2))


def cubes(kind):
    sizes = [lax.axis_size(axis) for axis in AXES]
    found = {}
    for place in np.ndindex(*sizes):
        corner = tuple((i + kind) // 2 % (size // 2) for i, size in zip(place, sizes))
        member = sum(mask * (i % 2) for mask, i in zip(MASK, place))
        found.setdefault(corner, {})[member] = int(np.ravel_multi_index(place, sizes))
    return [[members[i] for i in range(8)] for members in found.values()]


def heading_of(signs_by_axis):
    return tuple(signs_by_axis.get(axis, 0) for axis in range(3))


class Parity:
    def __init__(self, place):
        parities = [lax.rem(place[axis], 2) for axis in range(3)]
        self.even = [value == 0 for value in parities]
        self.position = sum(mask * value for mask, value in zip(MASK, parities))

    def choose(self, axes, values):
        if len(axes) == 1:
            return jnp.where(self.even[axes[0]], values(0), values(1))
        return jnp.where(
            self.even[axes[0]],
            jnp.where(self.even[axes[1]], values(0, 0), values(0, 1)),
            jnp.where(self.even[axes[1]], values(1, 0), values(1, 1)),
        )

    def own(self, y, axes, kinds):
        def value(*odd):
            return block(y, *heading_of({axis: 1 - 2 * (kind ^ i) for axis, kind, i in zip(axes, kinds, odd)}))

        return self.choose(axes, value)

    def toward(self, axes, signs, by_kinds):
        return self.choose(axes, lambda *odd: by_kinds[tuple(sign ^ i for sign, i in zip(signs, odd))])


def cube_b(y, parity):
    sent = []
    for axis in range(3):
        rest = [other for other in range(3) if other != axis]
        parts = [parity.own(y, (axis,), (1,))]
        for other in rest:
            first, second = sorted((axis, other))
            parts.append(parity.own(y, (first, second), (int(first == axis), int(second == axis))))
        sent.append((MASK[axis], jnp.concatenate(parts, axis=1)))
    for pair in PAIRS:
        sent.append((MASK[pair[0]] | MASK[pair[1]], parity.own(y, pair, (1, 1))))
    return sent


def members(got, parity):
    return {mask: got[parity.position ^ mask][:12] for mask in range(1, 7)}


def edge_at(tile, number):
    return tile[:, FACE + EDGE * number : FACE + EDGE * (number + 1)]


def passed(axis, other):
    return [i for i in range(3) if i != axis].index(other)


def cube_a(y, parity, from_b):
    sent = []
    for axis in range(3):
        parts = [parity.own(y, (axis,), (0,))]
        for other in range(3):
            if other != axis:
                parts.append(edge_at(from_b[MASK[other]], passed(other, axis)))
        sent.append((MASK[axis], jnp.concatenate(parts, axis=1)))
    for pair in PAIRS:
        sent.append((MASK[pair[0]] | MASK[pair[1]], parity.own(y, pair, (0, 0))))
    return sent


def cube_beside(parity, from_a, from_b):
    faces, edges = {}, {}
    for axis in range(3):
        by_kinds = {(0,): from_a[MASK[axis]][:, :FACE], (1,): from_b[MASK[axis]][:, :FACE]}
        for sign in range(2):
            faces[heading_of({axis: 1 - 2 * sign})] = parity.toward((axis,), (sign,), by_kinds)
    for pair in PAIRS:
        mask = MASK[pair[0]] | MASK[pair[1]]
        first, second = pair
        by_kinds = {
            (0, 0): from_a[mask][:, :EDGE],
            (1, 1): from_b[mask][:, :EDGE],
            (0, 1): edge_at(from_a[MASK[first]], passed(first, second)),
            (1, 0): edge_at(from_a[MASK[second]], passed(second, first)),
        }
        for signs in np.ndindex(2, 2):
            heading = heading_of({axis: 1 - 2 * sign for axis, sign in zip(pair, signs)})
            edges[heading] = parity.toward(pair, signs, by_kinds)
    return jnp.concatenate([{**faces, **edges}[heading] for heading in DIRECTIONS], axis=1)


def placed(sent, parity):
    blocks = {mask: value for mask, value in sent}
    return [(parity.position ^ mask, blocks.get(mask)) for mask in range(8)]


def cube_swap(kind, sent, live):
    sent, live = lax.optimization_barrier((sent, live))
    got = lax.all_to_all(sent, AXES, 0, 0, axis_index_groups=cubes(kind), tiled=True)
    return lax.optimization_barrier((got, live))


CUBE = jax.ShapeDtypeStruct((8, 16, 128), jnp.float32)


def exchange_by_cubes(sent, live):
    got, live = cube_swap(1, sent, live)
    live["from_b"] = got

    def second(y, from_b):
        parity = Parity(HERE)
        return (placed(cube_a(y[...], parity, members(from_b, parity)), parity),)

    (sent,) = kernel_call("cube_a", second, (CUBE,), live["y"], live["from_b"])
    got, live = cube_swap(0, sent, live)
    live["from_a"] = got
    return live


def from_cubes(from_a, from_b):
    parity = Parity(HERE)
    return cube_beside(parity, members(from_a, parity), members(from_b, parity))


def gathered(stage, axis, sent, live):
    sent, live = lax.optimization_barrier((sent, live))
    if stage < 2:
        got = lax.all_to_all(sent, AXES, 0, 0, axis_index_groups=lines_of(stage), tiled=True)
    else:
        got = lax.all_to_all(sent, axis, 0, 0, tiled=True)
    return lax.optimization_barrier((got, live))


def picked(got, place, stage, number):
    count = got.shape[0]
    here = line_place(stage)
    before = got[jnp.maximum(here - 1, 0)]
    after = got[jnp.minimum(here + 1, count - 1)]
    low = got[0, 12:16, :]
    for i in range(1, count):
        low = low + got[i, 12:16, :]
    rest = unfold(low)
    return before, after, [rest[:, 2 * EDGE + i : 2 * EDGE + i + 1] for i in range(number)]


def exchange_by_gathers(y, sent, place, number, live):
    sizes = [lax.axis_size(axis) for axis in AXES]

    def blocks(stage):
        return jax.ShapeDtypeStruct((sizes[stage], 16, 128), jnp.float32)

    live = dict(live, y=y)
    got, live = gathered(0, "gx", sent, live)

    def second(y, got, place):
        before, after, sums = picked(got, place, 0, number)
        ahead, behind = messages(1, y[...], unpack(before), unpack(after), None, None, sums)
        return spread(ahead, behind, line_place(1), sizes[1]), [before, after]

    sent, x_tiles = kernel_call("second_sum", second, (blocks(1), TILE), live["y"], got, HERE)
    live["x_tiles"] = x_tiles
    got, live = gathered(1, "gy", sent, live)

    def third(y, x_tiles, got, place):
        before, after, sums = picked(got, place, 1, number)
        ahead, behind = messages(2, y[...], *pair_of(x_tiles), unpack(before), unpack(after), sums)
        return spread(ahead, behind, line_place(2), sizes[2]), [before, after]

    sent, y_tiles = kernel_call("third_sum", third, (blocks(2), TILE), live["y"], live["x_tiles"], got, HERE)
    live["y_tiles"] = y_tiles
    return gathered(2, "gz", sent, live)


def from_gathers(got, x_tiles, y_tiles, place, number):
    before, after, sums = picked(got, place, 2, number)
    return beside(*pair_of(x_tiles), *pair_of(y_tiles), unpack(before), unpack(after)), sums


def load_call(loads, counts, signs, shapes):
    def kernel(loads_in, counts_in, signs_in, y, sent, alive, signed, lines, counts, signs, arrived):
        copies = [
            pltpu.make_async_copy(source, target, arrived.at[i])
            for i, (source, target) in enumerate(((loads_in, lines), (counts_in, counts), (signs_in, signs)))
        ]
        for copy in copies:
            copy.start()
        copies[0].wait()
        cases = y.shape[0]
        folds = y.shape[1] // 128
        values = jnp.concatenate([lines[pl.ds(i, cases, stride=folds), :] for i in range(folds)], axis=1)
        y[...] = values
        parity = Parity(HERE)
        store_blocks(sent, placed(cube_b(values, parity), parity))
        copies[1].wait()
        position = lax.broadcasted_iota(jnp.int32, (1, FACE), 1)
        alive[...] = jnp.concatenate(
            [
                (position[:, : CAPACITY[course]] < counts[:, course : course + 1]).astype(jnp.float32)
                for course in range(len(DIRECTIONS))
            ],
            axis=1,
        )
        copies[2].wait()
        signed[...] = signs[...].astype(jnp.float32) * alive[...]

    return pl.pallas_call(
        kernel,
        name="load_blocks",
        in_specs=[pl.BlockSpec(memory_space=pl.ANY) for _ in range(3)],
        out_specs=[pl.BlockSpec(memory_space=pltpu.VMEM) for _ in shapes],
        out_shape=[pltpu.VMEM(shape.shape, shape.dtype) for shape in shapes],
        scratch_shapes=[
            pltpu.VMEM(loads.shape, loads.dtype),
            pltpu.VMEM(counts.shape, counts.dtype),
            pltpu.VMEM(signs.shape, signs.dtype),
            pltpu.SemaphoreType.DMA((3,)),
        ],
    )(loads, counts, signs)


def per_device(loads, dual_ops, precond, counts, signs):
    place = HERE
    dual, pre = dual_ops[0, 0, 0], precond[0, 0, 0]
    loads = loads[0, 0, 0]
    sizes = [lax.axis_size(axis) for axis in AXES]
    vector = jax.ShapeDtypeStruct(loads.shape, jnp.float32)
    rounded = jax.ShapeDtypeStruct(loads.shape, jnp.bfloat16)
    column = jax.ShapeDtypeStruct((loads.shape[0], 1), jnp.float32)
    first_blocks = jax.ShapeDtypeStruct((sizes[0], 16, 128), jnp.float32)

    def times(scaled, matrix):
        return jnp.dot(scaled, matrix, preferred_element_type=jnp.float32)

    def dot(left, right):
        return jnp.sum(left * right, axis=1, keepdims=True)

    row = jax.ShapeDtypeStruct((1, loads.shape[1]), jnp.float32)
    live = dict(dual=dual, pre=pre)
    live["y"], sent, live["alive"], live["signed"] = load_call(
        loads.reshape(-1, 128), counts[0, 0], signs[0, 0], (vector, CUBE, row, row)
    )
    live = exchange_by_cubes(sent, live)

    def assemble(y, alive, signed, from_a, from_b):
        whole = alive[...] * (y[...] + from_cubes(from_a, from_b))
        return whole, (signed[...] * whole).astype(jnp.bfloat16)

    names = ("y", "alive", "signed", "from_a", "from_b")
    live["residual"], scaled = kernel_call("begin", assemble, (vector, rounded), *[live.pop(name) if name[0] in "fy" else live[name] for name in names])

    def precond_blocks(product, signed, residual):
        y = signed[...] * product[...]
        parity = Parity(HERE)
        return y, dot(residual[...], y), placed(cube_b(y, parity), parity)

    live["y"], live["gamma_part"], sent = kernel_call(
        "precond_blocks",
        precond_blocks,
        (vector, column, CUBE),
        times(scaled, live["pre"]),
        live["signed"],
        live["residual"],
    )
    live = exchange_by_cubes(sent, live)
    live["direction"], scaled = kernel_call("aim", assemble, (vector, rounded), *[live.pop(name) if name[0] in "fy" else live[name] for name in names])

    def image_blocks(product, signed, direction, gamma_part, place):
        y = signed[...] * product[...]
        sums = (gamma_part[...], dot(direction[...], y))
        y = turned(y)
        return y, spread(*messages(0, y, None, None, None, None, sums), line_place(0), sizes[0])

    y, sent = kernel_call(
        "image_blocks",
        image_blocks,
        (vector, first_blocks),
        times(scaled, live["dual"]),
        live["signed"],
        live["direction"],
        live.pop("gamma_part"),
        place,
    )
    got, live = exchange_by_gathers(y, sent, place, 2, live)

    def first_step(got, x_tiles, y_tiles, y, place, alive, signed, direction, residual):
        near, (gamma, curvature) = from_gathers(got, x_tiles, y_tiles, place, 2)
        image = alive[...] * turned(y[...] + near)
        step = gamma / curvature
        left = residual[...] - step * image
        return step * direction[...], left, (signed[...] * left).astype(jnp.bfloat16), gamma

    names = ("x_tiles", "y_tiles", "y", "place", "alive", "signed", "direction", "residual")
    live["multipliers"], live["residual"], scaled, live["gamma"] = kernel_call(
        "first_step", first_step, (vector, vector, rounded, column), got, *[live[name] if name != "place" else HERE for name in names]
    )

    def sum_blocks(product, signed, left, place):
        y = signed[...] * product[...]
        sums = (dot(left[...], y),)
        y = turned(y)
        return y, spread(*messages(0, y, None, None, None, None, sums), line_place(0), sizes[0])

    for iteration in range(1, ITERS):
        y, sent = kernel_call(
            "smooth_blocks",
            sum_blocks,
            (vector, first_blocks),
            times(scaled, live["pre"]),
            live["signed"],
            live["residual"],
            HERE,
        )
        got, live = exchange_by_gathers(y, sent, HERE, 1, live)

        def turn(got, x_tiles, y_tiles, y, place, alive, signed, direction, gamma_old):
            near, (gamma,) = from_gathers(got, x_tiles, y_tiles, place, 1)
            smoothed = alive[...] * turned(y[...] + near)
            fresh = smoothed + (gamma / gamma_old[...]) * direction[...]
            return fresh, (signed[...] * fresh).astype(jnp.bfloat16), gamma

        names = ("x_tiles", "y_tiles", "y", "place", "alive", "signed", "direction", "gamma")
        live["direction"], scaled, live["gamma"] = kernel_call(
            "turn", turn, (vector, rounded, column), got, *[live[name] if name != "place" else HERE for name in names]
        )
        y, sent = kernel_call(
            "sum_blocks",
            sum_blocks,
            (vector, first_blocks),
            times(scaled, live["dual"]),
            live["signed"],
            live["direction"],
            HERE,
        )
        got, live = exchange_by_gathers(y, sent, HERE, 1, live)

        def advance(got, x_tiles, y_tiles, y, place, alive, signed, direction, gamma, multipliers, residual):
            near, (curvature,) = from_gathers(got, x_tiles, y_tiles, place, 1)
            image = alive[...] * turned(y[...] + near)
            step = gamma[...] / curvature
            left = residual[...] - step * image
            results = (multipliers[...] + step * direction[...], left)
            if iteration < ITERS - 1:
                results += ((signed[...] * left).astype(jnp.bfloat16),)
            return results

        lines = jax.ShapeDtypeStruct((loads.size // 128, 128), jnp.float32)
        shapes = (vector, vector, rounded) if iteration < ITERS - 1 else (lines, lines)
        names = ("x_tiles", "y_tiles", "y", "place", "alive", "signed", "direction", "gamma", "multipliers", "residual")
        live["multipliers"], live["residual"], *rest = kernel_call(
            "advance",
            advance,
            shapes,
            got,
            *[live[name] if name != "place" else HERE for name in names],
            last=iteration == ITERS - 1,
        )
        if rest:
            scaled = rest[0]
    whole = (1, 1, 1, *loads.shape)
    return (live["multipliers"].reshape(whole), live["residual"].reshape(whole))


def solution(mesh):
    placed = (
        P("gx", "gy", "gz", None, None),
        P("gx", "gy", "gz", None, None),
        P("gx", "gy", "gz", None, None),
        P("gx", "gy", "gz", None),
        P("gx", "gy", "gz", None),
    )
    return jax.shard_map(
        per_device,
        mesh=mesh,
        in_specs=placed,
        out_specs=(P("gx", "gy", "gz", None, None), P("gx", "gy", "gz", None, None)),
        check_vma=False,
    )
```
